32 devices in a mesh: dp: 2 (over core), space: 16 (over z, y, x).
Axes of the slice: x: 2, y: 2, z: 4, core: 2. Of those that a mesh axis runs over, the one named last changes fastest.
Arguments:
- features: bfloat16 [32, 2304, 2048], P('dp', 'space'), parts along dimension 0, may hold values from 0 to 18
- depth_weights: bfloat16 [3, 9, 2048], replicated, may hold values from -2 to 2
- point_weights: bfloat16 [3, 2048, 256], replicated, may hold values from -0.125 to 0.125
- branch_weight: bfloat16 [2048, 256], replicated, may hold values from -0.125 to 0.125
- pooling_weight: bfloat16 [2048, 256], replicated, may hold values from -0.125 to 0.125
- project_weight: bfloat16 [1280, 256], replicated, may hold values from -0.15625 to 0.15625
- refine_depth: bfloat16 [9, 256], replicated, may hold values from -2 to 2
- refine_point: bfloat16 [256, 256], replicated, may hold values from -0.375 to 0.375
Outputs:
- refined: bfloat16 [32, 2304, 256], P('dp', 'space'), parts along dimension 0
The draws below stay inside these ranges and needn't reach their ends.
There are 2 independent parts, one for each index of `dp`. The reference program is written for one: setup_inputs(seed, part) draws one part's arguments, and reference() takes and returns one part's arrays. A program takes and returns all parts, laid end to end along the dimension named above; an argument that names none is the same for every part. Nothing has to cross between parts.
All inputs are finite; a program needn't handle non-finite values.
Results may differ from the reference program's by a relative error of at most 0.0066.
Values may be sent and summed in bfloat16 or wider, within the bound.
No kernel may reach another device: no remote copies, remote signals or barrier semaphores. Data moves between devices by JAX's collectives and lax.ppermute only.
A program may use at most 128 MiB of HBM per device.

```python
import math
import jax
import jax.numpy as jnp
from jax import lax

C_IN = 2048
C_OUT = 256
RATE_LOW = 12
RATE_MID = 24
RATE_HIGH = 36
ROWS = 48
COLS = 48
IMAGES = 16


def draw_features(key, part):
    first, second = jax.random.split(jax.random.fold_in(key, 11), 2)
    shape = (IMAGES, ROWS * COLS, C_IN)
    base = jnp.exp(jax.random.uniform(first, shape, jnp.float32, math.log(0.05), math.log(2.0)))
    channel = jnp.exp(jax.random.uniform(second, (C_IN,), jnp.float32, math.log(0.3), math.log(3.0)))
    ramp = 3.0 ** (jnp.arange(ROWS * COLS, dtype=jnp.float32) / max(ROWS * COLS - 1, 1))
    values = base * ramp[None, :, None] * channel
    return jnp.minimum(values, 18.0).astype(jnp.bfloat16)


def normal_values(key, extent, scale, most, kind=jnp.bfloat16):
    array = jax.random.normal(key, extent, jnp.float32) * scale
    return jnp.minimum(jnp.maximum(array, -most), most).astype(kind)


def setup_inputs(seed: int = 0, part: int = 0) -> dict:
    key_of = jax.random.split(jax.random.key(seed), 9)
    part_splits = jax.random.split(jax.random.fold_in(key_of[8], part), 9)
    return {
        "features": draw_features(jax.random.fold_in(jax.random.fold_in(key_of[8], part), 71), part),
        "depth_weights": normal_values(key_of[1], (3, 9, C_IN), 9 ** -0.5, 2.0),
        "point_weights": normal_values(key_of[2], (3, C_IN, C_OUT), C_IN ** -0.5, 0.125),
        "branch_weight": normal_values(key_of[3], (C_IN, C_OUT), C_IN ** -0.5, 0.125),
        "pooling_weight": normal_values(key_of[4], (C_IN, C_OUT), C_IN ** -0.5, 0.125),
        "project_weight": normal_values(key_of[5], (5 * C_OUT, C_OUT), (5 * C_OUT) ** -0.5, 0.15625),
        "refine_depth": normal_values(key_of[6], (9, C_OUT), 9 ** -0.5, 2.0),
        "refine_point": normal_values(key_of[7], (C_OUT, C_OUT), C_OUT ** -0.5, 0.375),
    }


def depthwise(image, taps, rate):
    padded = jnp.pad(image, ((rate, rate), (rate, rate), (0, 0)))
    height = image.shape[0]
    width = image.shape[1]
    total = jnp.zeros(image.shape, jnp.float32)
    for row in range(3):
        for col in range(3):
            window = padded[row * rate:row * rate + height, col * rate:col * rate + width, :]
            total = total + window.astype(jnp.float32) * taps[3 * row + col].astype(jnp.float32)
    return jax.nn.relu(total).astype(jnp.bfloat16)


def pointwise(image, weight):
    flat = image.reshape(-1, image.shape[-1])
    product = jnp.dot(flat, weight, preferred_element_type=jnp.float32)
    return jax.nn.relu(product).reshape(image.shape[:-1] + (weight.shape[1],)).astype(jnp.bfloat16)


def reference(features, depth_weights, point_weights, branch_weight, pooling_weight, project_weight, refine_depth, refine_point):
    rates = (RATE_LOW, RATE_MID, RATE_HIGH)

    def one_image(flat):
        image = flat.reshape(ROWS, COLS, flat.shape[-1])
        pooled = jnp.mean(flat.astype(jnp.float32), axis=0)
        branches = [pointwise(image, branch_weight)]
        for index in range(3):
            spread = depthwise(image, depth_weights[index], rates[index])
            branches.append(pointwise(spread, point_weights[index]))
        pool_vector = jax.nn.relu(jnp.dot(pooled.astype(jnp.bfloat16)[None, :], pooling_weight, preferred_element_type=jnp.float32)).astype(jnp.bfloat16)
        branches.append(jnp.broadcast_to(pool_vector[0][None, None, :], (ROWS, COLS, pool_vector.shape[1])))
        context = pointwise(jnp.concatenate(branches, axis=-1), project_weight)
        spread = depthwise(context, refine_depth, 1)
        return pointwise(spread, refine_point).reshape(ROWS * COLS, refine_point.shape[1])

    return lax.map(one_image, features)
```

```python
import functools

import jax
import jax.numpy as jnp
from jax import lax
from jax.experimental import pallas as pl
from jax.experimental.pallas import tpu as pltpu
from jax.sharding import PartitionSpec as P

ROWS = 48
COLS = 48
RATE = 12
BANDS = ROWS // RATE
CLASSES = 4
CLASS_ROWS = RATE // CLASSES
BLOCK = CLASS_ROWS * COLS
TILE = 512
HALF = 256
WINDOW = 4
ORDER = (0, 1, 3, 2)
HOPS = (2, 3, 1, 0)
F32 = jnp.float32
BF16 = jnp.bfloat16


def load_tile(info, x_refs, plain, shifted, raw):
    width = plain.shape[-1]

    @pl.when(pl.program_id(0) == 0)
    def _():
        shifted[:, :, 0:8, :] = jnp.zeros((BANDS, CLASS_ROWS, 8, width), F32)
        shifted[:, :, 48:56, :] = jnp.zeros((BANDS, CLASS_ROWS, 8, width), F32)

    for hop in range(BANDS):
        band = jnp.bitwise_xor(info[0], hop)
        block = x_refs[hop][...]
        raw[band] = block
        wide = block.astype(F32).reshape(CLASS_ROWS, COLS, width)
        plain[band] = wide
        shifted[band, :, 4:52, :] = wide


def spread_rows(plain, shifted, taps, spread, row, lane):
    lanes = pl.ds(lane, HALF)
    for branch in range(3):
        weights = [taps[9 * branch + tap, :, lanes] for tap in range(9)]
        for band in range(BANDS):
            tiles = []
            for tile in range(COLS // 8):
                total = None
                for up in (-1, 0, 1):
                    source = band + up * (branch + 1)
                    if not 0 <= source < BANDS:
                        continue
                    for side in (-1, 0, 1):
                        shift = side * RATE * (branch + 1)
                        if 8 * tile + shift + 7 < 0 or 8 * tile + shift >= COLS:
                            continue
                        if shift % 8 == 0:
                            value = plain[source, row, 8 * tile + shift:8 * tile + shift + 8, lanes]
                        else:
                            start = 8 * tile + shift + 4
                            value = shifted[source, row, start:start + 8, lanes]
                        term = value * weights[3 * (up + 1) + (side + 1)]
                        total = term if total is None else total + term
                tiles.append(jnp.maximum(total, 0.0))
            sums = jnp.concatenate(tiles, axis=0).astype(BF16)
            spread[branch, band, pl.ds(pl.multiple_of(row * COLS, COLS), COLS), lanes] = sums


def pyramid_tile(info, x_refs, taps, point, branch, plain, shifted, raw, spread, sums):
    width = plain.shape[-1]
    load_tile(info, x_refs, plain, shifted, raw)

    def step(index, carry):
        spread_rows(plain, shifted, taps, spread, index // (width // HALF),
                    pl.multiple_of((index % (width // HALF)) * HALF, HALF))
        return carry

    lax.fori_loop(0, CLASS_ROWS * (width // HALF), step, 0)
    cells = BANDS * BLOCK
    parts = [jnp.dot(raw[...].reshape(cells, width), branch[...], preferred_element_type=F32)]
    for index in range(3):
        parts.append(
            jnp.dot(spread[index].reshape(cells, width), point[index], preferred_element_type=F32)
        )

    @pl.when(pl.program_id(0) == 0)
    def _():
        for index in range(4):
            sums[index] = parts[index]

    @pl.when(pl.program_id(0) > 0)
    def _():
        for index in range(4):
            sums[index] += parts[index]


def channel_sum(plain):
    width = plain.shape[-1]
    total = jnp.sum(plain[...].reshape(BANDS * BLOCK // 8, 8, width), axis=0)
    return total


def project(sums, weight):
    total = None
    for index in range(4):
        joined = jnp.maximum(sums[index], 0.0).astype(BF16)
        term = jnp.dot(
            joined, weight[HALF * index:HALF * (index + 1), :], preferred_element_type=F32
        )
        total = term if total is None else total + term
    return total


def class_kernel(info, x0, x1, x2, x3, taps, point, branch, weight, out, channel, plain, shifted,
                 raw, spread, sums):
    pyramid_tile(info, (x0, x1, x2, x3), taps, point, branch, plain, shifted, raw, spread, sums)
    channel[...] = channel_sum(plain)

    @pl.when(pl.program_id(0) == pl.num_programs(0) - 1)
    def _():
        out[...] = project(sums, weight)


def last_kernel(info, x0, x1, x2, x3, taps, point, branch, weight, pooling, channel0, channel1,
                channel2, pre0, pre1, pre2, refine_taps, refine_point, out, plain, shifted, raw,
                spread, sums, pool, context, rows):
    pyramid_tile(info, (x0, x1, x2, x3), taps, point, branch, plain, shifted, raw, spread, sums)
    total = channel0[...] + channel1[...] + channel2[...] + channel_sum(plain)
    mean = jnp.sum(total, axis=0, keepdims=True) * (1.0 / (ROWS * COLS))
    mean = jnp.broadcast_to(mean, (16, mean.shape[1])).astype(BF16)
    term = jnp.dot(mean, pooling[...], preferred_element_type=F32)

    @pl.when(pl.program_id(0) == 0)
    def _():
        pool[...] = term
        context[...] = jnp.zeros(context.shape, F32)

    @pl.when(pl.program_id(0) > 0)
    def _():
        pool[...] += term

    @pl.when(pl.program_id(0) == pl.num_programs(0) - 1)
    def _():
        vector = jnp.maximum(pool[...], 0.0).astype(BF16)
        bias = jnp.dot(vector, weight[4 * HALF:5 * HALF, :], preferred_element_type=F32)[0:1, :]
        pres = (pre0[...], pre1[...], pre2[...], project(sums, weight))
        for index, pre in enumerate(pres):
            first = CLASS_ROWS * jnp.bitwise_xor(info[1], ORDER[index])
            value = jnp.maximum(pre + bias, 0.0).astype(BF16).astype(F32)
            value = value.reshape(BANDS, CLASS_ROWS, COLS, HALF)
            for band in range(BANDS):
                for row in range(CLASS_ROWS):
                    context[RATE * band + first + row + 1, 8:56, :] = value[band, row]

        def step(row, carry):
            total = None
            for up in range(3):
                for side in range(3):
                    term = context[row + up, 7 + side:7 + side + COLS, :] * jnp.concatenate(
                        [refine_taps[3 * up + side]] * (COLS // 8), axis=0
                    )
                    total = term if total is None else total + term
            rows[pl.ds(pl.multiple_of(row * COLS, COLS), COLS), :] = jnp.maximum(total, 0.0).astype(BF16)
            return carry

        lax.fori_loop(0, ROWS, step, 0)
        product = jnp.dot(rows[...], refine_point[...], preferred_element_type=F32)
        out[...] = jnp.maximum(product, 0.0).astype(BF16)


def whole(shape):
    return pl.BlockSpec(shape, lambda i, info: (0,) * len(shape))


def pyramid_specs(channels):
    specs = [pl.BlockSpec((BLOCK, TILE), lambda i, info: (0, i)) for _ in range(BANDS)]
    specs.append(pl.BlockSpec((27, 8, TILE), lambda i, info: (0, 0, i)))
    specs.append(pl.BlockSpec((3, TILE, HALF), lambda i, info: (0, i, 0)))
    specs.append(pl.BlockSpec((TILE, HALF), lambda i, info: (i, 0)))
    specs.append(whole((5 * HALF, HALF)))
    return specs


def pyramid_scratch():
    return [
        pltpu.VMEM((BANDS, CLASS_ROWS, COLS, TILE), F32),
        pltpu.VMEM((BANDS, CLASS_ROWS, COLS + 8, TILE), F32),
        pltpu.VMEM((BANDS, BLOCK, TILE), BF16),
        pltpu.VMEM((3, BANDS, BLOCK, TILE), BF16),
        pltpu.VMEM((4, BANDS * BLOCK, HALF), F32),
    ]


PARAMS = pltpu.CompilerParams(
    dimension_semantics=("arbitrary",), vmem_limit_bytes=52 * 1024 * 1024
)


def class_call(info, blocks, taps, point, branch, weight):
    channels = blocks[0].shape[1]
    return pl.pallas_call(
        class_kernel,
        grid_spec=pltpu.PrefetchScalarGridSpec(
            num_scalar_prefetch=1,
            grid=(channels // TILE,),
            in_specs=pyramid_specs(channels),
            out_specs=[
                whole((BANDS * BLOCK, HALF)),
                pl.BlockSpec((8, TILE), lambda i, info: (0, i)),
            ],
            scratch_shapes=pyramid_scratch(),
        ),
        out_shape=[
            jax.ShapeDtypeStruct((BANDS * BLOCK, HALF), F32),
            jax.ShapeDtypeStruct((8, channels), F32),
        ],
        compiler_params=PARAMS,
        name="pyramid_class",
    )(info, *blocks, taps, point, branch, weight)


def last_call(info, blocks, taps, point, branch, weight, pooling, channel, pres, refine_taps, refine_point):
    channels = blocks[0].shape[1]
    specs = pyramid_specs(channels)
    specs.append(pl.BlockSpec((TILE, HALF), lambda i, info: (i, 0)))
    specs += [pl.BlockSpec((8, TILE), lambda i, info: (0, i)) for _ in range(3)]
    specs += [whole((BANDS * BLOCK, HALF)) for _ in range(3)]
    specs += [whole((9, 8, HALF)), whole((HALF, HALF))]
    return pl.pallas_call(
        last_kernel,
        grid_spec=pltpu.PrefetchScalarGridSpec(
            num_scalar_prefetch=1,
            grid=(channels // TILE,),
            in_specs=specs,
            out_specs=whole((ROWS * COLS, HALF)),
            scratch_shapes=pyramid_scratch() + [
                pltpu.VMEM((16, HALF), F32),
                pltpu.VMEM((ROWS + 2, COLS + 16, HALF), F32),
                pltpu.VMEM((ROWS * COLS, HALF), BF16),
            ],
        ),
        out_shape=jax.ShapeDtypeStruct((ROWS * COLS, HALF), BF16),
        compiler_params=PARAMS,
        name="pyramid_last",
    )(info, *blocks, taps, point, branch, weight, pooling, *channel, *pres, refine_taps, refine_point)


def exchange(features):
    parts = lax.axis_size("space")
    block = features.shape[1]
    channels = features.shape[2]
    sub = BLOCK // block
    me = lax.axis_index("space").astype(jnp.int32)
    sent = []
    classes = []
    for kind in ORDER:
        blocks = {}
        for hop in HOPS:
            pieces = []
            for piece in range(sub):
                distance = (hop * CLASSES + kind) * sub + piece
                target = jnp.bitwise_xor(me, distance)
                if distance and len(sent) >= WINDOW:
                    target, _ = lax.optimization_barrier((target, sent[len(sent) - WINDOW]))
                value = lax.dynamic_slice_in_dim(features, target, 1, 0)
                if distance:
                    value = lax.ppermute(value, "space", [(i, i ^ distance) for i in range(parts)])
                    sent.append(value)
                pieces.append(value.reshape(block, channels))
            if sub == 1:
                blocks[hop] = pieces[0]
            else:
                joined = jnp.zeros((BLOCK, channels), features.dtype)
                for piece in range(sub):
                    start = jnp.bitwise_xor(me % sub, piece) * block
                    joined = lax.dynamic_update_slice(joined, pieces[piece], (start, 0))
                blocks[hop] = joined
        classes.append([blocks[hop] for hop in range(BANDS)])
    return me, sub, classes


def body(
    features,
    depth_weights,
    point_weights,
    branch_weight,
    pooling_weight,
    project_weight,
    refine_depth,
    refine_point,
):
    parts = lax.axis_size("space")
    assert features.shape[0] == parts
    block = features.shape[1]
    channels = features.shape[2]
    taps = jnp.broadcast_to(depth_weights.reshape(27, 1, channels).astype(F32), (27, 8, channels))
    refine_taps = jnp.broadcast_to(refine_depth.reshape(9, 1, HALF).astype(F32), (9, 8, HALF))
    me, sub, classes = exchange(features)
    info = jnp.stack([me // (CLASSES * sub), (me // sub) % CLASSES])
    shared = (taps, point_weights, branch_weight, project_weight)
    pres = []
    channel = []
    for blocks in classes[:3]:
        pre, total = class_call(info, blocks, *shared)
        pres.append(pre)
        channel.append(total)
    refined = last_call(
        info, classes[3], *shared, pooling_weight, channel, pres, refine_taps, refine_point
    )
    return lax.all_to_all(refined.reshape(parts, block, HALF), "space", 0, 0, tiled=True)


def solution(mesh):
    return jax.shard_map(
        body,
        mesh=mesh,
        in_specs=(P("dp", "space", None), P(), P(), P(), P(), P(), P(), P()),
        out_specs=P("dp", "space", None),
        check_vma=False,
    )
```

```python
import functools

import jax
import jax.numpy as jnp
from jax import lax
from jax.experimental import pallas as pl
from jax.experimental.pallas import tpu as pltpu
from jax.sharding import PartitionSpec as P

ROWS = 48
COLS = 48
RATE = 12
BANDS = ROWS // RATE
CLASSES = 4
CLASS_ROWS = RATE // CLASSES
BLOCK = CLASS_ROWS * COLS
TILE = 512
HALF = 256
WINDOW = 4
ORDER = (0, 1, 3, 2)
HOPS = (2, 3, 1, 0)
F32 = jnp.float32
BF16 = jnp.bfloat16


def load_tile(info, x_refs, plain, shifted, raw):
    width = plain.shape[-1]

    @pl.when(pl.program_id(0) == 0)
    def _():
        shifted[:, :, 0:8, :] = jnp.zeros((BANDS, CLASS_ROWS, 8, width), F32)
        shifted[:, :, 48:56, :] = jnp.zeros((BANDS, CLASS_ROWS, 8, width), F32)

    for hop in range(BANDS):
        band = jnp.bitwise_xor(info[0], hop)
        block = x_refs[hop][...]
        raw[band] = block
        wide = block.astype(F32).reshape(CLASS_ROWS, COLS, width)
        plain[band] = wide
        shifted[band, :, 4:52, :] = wide


def spread_rows(plain, shifted, taps, spread, row, lane):
    lanes = pl.ds(lane, HALF)
    for branch in range(3):
        weights = [taps[9 * branch + tap, :, lanes] for tap in range(9)]
        for band in range(BANDS):
            tiles = []
            for tile in range(COLS // 8):
                total = None
                for up in (-1, 0, 1):
                    source = band + up * (branch + 1)
                    if not 0 <= source < BANDS:
                        continue
                    for side in (-1, 0, 1):
                        shift = side * RATE * (branch + 1)
                        if 8 * tile + shift + 7 < 0 or 8 * tile + shift >= COLS:
                            continue
                        if shift % 8 == 0:
                            value = plain[source, row, 8 * tile + shift:8 * tile + shift + 8, lanes]
                        else:
                            start = 8 * tile + shift + 4
                            value = shifted[source, row, start:start + 8, lanes]
                        term = value * weights[3 * (up + 1) + (side + 1)]
                        total = term if total is None else total + term
                tiles.append(jnp.maximum(total, 0.0))
            sums = jnp.concatenate(tiles, axis=0).astype(BF16)
            spread[branch, band, pl.ds(pl.multiple_of(row * COLS, COLS), COLS), lanes] = sums


def pyramid_tile(info, x_refs, taps, point, branch, plain, shifted, raw, spread, sums):
    width = plain.shape[-1]
    load_tile(info, x_refs, plain, shifted, raw)

    def step(index, carry):
        spread_rows(plain, shifted, taps, spread, index // (width // HALF),
                    pl.multiple_of((index % (width // HALF)) * HALF, HALF))
        return carry

    lax.fori_loop(0, CLASS_ROWS * (width // HALF), step, 0)
    cells = BANDS * BLOCK
    parts = [jnp.dot(raw[...].reshape(cells, width), branch[...], preferred_element_type=F32)]
    for index in range(3):
        parts.append(
            jnp.dot(spread[index].reshape(cells, width), point[index], preferred_element_type=F32)
        )

    @pl.when(pl.program_id(0) == 0)
    def _():
        for index in range(4):
            sums[index] = parts[index]

    @pl.when(pl.program_id(0) > 0)
    def _():
        for index in range(4):
            sums[index] += parts[index]


def channel_sum(plain):
    width = plain.shape[-1]
    total = jnp.sum(plain[...].reshape(BANDS * BLOCK // 8, 8, width), axis=0)
    return total


def project(sums, weight):
    total = None
    for index in range(4):
        joined = jnp.maximum(sums[index], 0.0).astype(BF16)
        term = jnp.dot(
            joined, weight[HALF * index:HALF * (index + 1), :], preferred_element_type=F32
        )
        total = term if total is None else total + term
    return total


def class_kernel(info, x0, x1, x2, x3, taps, point, branch, weight, out, channel, plain, shifted,
                 raw, spread, sums):
    pyramid_tile(info, (x0, x1, x2, x3), taps, point, branch, plain, shifted, raw, spread, sums)
    channel[...] = channel_sum(plain)

    @pl.when(pl.program_id(0) == pl.num_programs(0) - 1)
    def _():
        out[...] = project(sums, weight)


def last_kernel(info, x0, x1, x2, x3, taps, point, branch, weight, pooling, channel0, channel1,
                channel2, pre0, pre1, pre2, refine_taps, refine_point, out, plain, shifted, raw,
                spread, sums, pool, context, rows):
    pyramid_tile(info, (x0, x1, x2, x3), taps, point, branch, plain, shifted, raw, spread, sums)
    total = channel0[...] + channel1[...] + channel2[...] + channel_sum(plain)
    mean = jnp.sum(total, axis=0, keepdims=True) * (1.0 / (ROWS * COLS))
    mean = jnp.broadcast_to(mean, (16, mean.shape[1])).astype(BF16)
    term = jnp.dot(mean, pooling[...], preferred_element_type=F32)

    @pl.when(pl.program_id(0) == 0)
    def _():
        pool[...] = term
        context[...] = jnp.zeros(context.shape, F32)

    @pl.when(pl.program_id(0) > 0)
    def _():
        pool[...] += term

    @pl.when(pl.program_id(0) == pl.num_programs(0) - 1)
    def _():
        vector = jnp.maximum(pool[...], 0.0).astype(BF16)
        bias = jnp.dot(vector, weight[4 * HALF:5 * HALF, :], preferred_element_type=F32)[0:1, :]
        pres = (pre0[...], pre1[...], pre2[...], project(sums, weight))
        for index, pre in enumerate(pres):
            first = CLASS_ROWS * jnp.bitwise_xor(info[1], ORDER[index])
            value = jnp.maximum(pre + bias, 0.0).astype(BF16).astype(F32)
            value = value.reshape(BANDS, CLASS_ROWS, COLS, HALF)
            for band in range(BANDS):
                for row in range(CLASS_ROWS):
                    context[RATE * band + first + row + 1, 8:56, :] = value[band, row]

        def step(row, carry):
            total = None
            for up in range(3):
                for side in range(3):
                    term = context[row + up, 7 + side:7 + side + COLS, :] * jnp.concatenate(
                        [refine_taps[3 * up + side]] * (COLS // 8), axis=0
                    )
                    total = term if total is None else total + term
            rows[pl.ds(pl.multiple_of(row * COLS, COLS), COLS), :] = jnp.maximum(total, 0.0).astype(BF16)
            return carry

        lax.fori_loop(0, ROWS, step, 0)
        product = jnp.dot(rows[...], refine_point[...], preferred_element_type=F32)
        out[...] = jnp.maximum(product, 0.0).astype(BF16)


def whole(shape):
    return pl.BlockSpec(shape, lambda i, info: (0,) * len(shape))


def pyramid_specs(channels):
    specs = [pl.BlockSpec((BLOCK, TILE), lambda i, info: (0, i)) for _ in range(BANDS)]
    specs.append(pl.BlockSpec((27, 8, TILE), lambda i, info: (0, 0, i)))
    specs.append(pl.BlockSpec((3, TILE, HALF), lambda i, info: (0, i, 0)))
    specs.append(pl.BlockSpec((TILE, HALF), lambda i, info: (i, 0)))
    specs.append(whole((5 * HALF, HALF)))
    return specs


def pyramid_scratch():
    return [
        pltpu.VMEM((BANDS, CLASS_ROWS, COLS, TILE), F32),
        pltpu.VMEM((BANDS, CLASS_ROWS, COLS + 8, TILE), F32),
        pltpu.VMEM((BANDS, BLOCK, TILE), BF16),
        pltpu.VMEM((3, BANDS, BLOCK, TILE), BF16),
        pltpu.VMEM((4, BANDS * BLOCK, HALF), F32),
    ]


PARAMS = pltpu.CompilerParams(
    dimension_semantics=("arbitrary",), vmem_limit_bytes=52 * 1024 * 1024
)


def class_call(info, blocks, taps, point, branch, weight):
    channels = blocks[0].shape[1]
    return pl.pallas_call(
        class_kernel,
        grid_spec=pltpu.PrefetchScalarGridSpec(
            num_scalar_prefetch=1,
            grid=(channels // TILE,),
            in_specs=pyramid_specs(channels),
            out_specs=[
                whole((BANDS * BLOCK, HALF)),
                pl.BlockSpec((8, TILE), lambda i, info: (0, i)),
            ],
            scratch_shapes=pyramid_scratch(),
        ),
        out_shape=[
            jax.ShapeDtypeStruct((BANDS * BLOCK, HALF), F32),
            jax.ShapeDtypeStruct((8, channels), F32),
        ],
        compiler_params=PARAMS,
        name="pyramid_class",
    )(info, *blocks, taps, point, branch, weight)


def last_call(info, blocks, taps, point, branch, weight, pooling, channel, pres, refine_taps, refine_point):
    channels = blocks[0].shape[1]
    specs = pyramid_specs(channels)
    specs.append(pl.BlockSpec((TILE, HALF), lambda i, info: (i, 0)))
    specs += [pl.BlockSpec((8, TILE), lambda i, info: (0, i)) for _ in range(3)]
    specs += [whole((BANDS * BLOCK, HALF)) for _ in range(3)]
    specs += [whole((9, 8, HALF)), whole((HALF, HALF))]
    return pl.pallas_call(
        last_kernel,
        grid_spec=pltpu.PrefetchScalarGridSpec(
            num_scalar_prefetch=1,
            grid=(channels // TILE,),
            in_specs=specs,
            out_specs=whole((ROWS * COLS, HALF)),
            scratch_shapes=pyramid_scratch() + [
                pltpu.VMEM((16, HALF), F32),
                pltpu.VMEM((ROWS + 2, COLS + 16, HALF), F32),
                pltpu.VMEM((ROWS * COLS, HALF), BF16),
            ],
        ),
        out_shape=jax.ShapeDtypeStruct((ROWS * COLS, HALF), BF16),
        compiler_params=PARAMS,
        name="pyramid_last",
    )(info, *blocks, taps, point, branch, weight, pooling, *channel, *pres, refine_taps, refine_point)


def exchange(features, consume):
    parts = lax.axis_size("space")
    block = features.shape[1]
    channels = features.shape[2]
    sub = BLOCK // block
    me = lax.axis_index("space").astype(jnp.int32)
    first = None
    values = {}
    for kind in ORDER:
        origin = me
        if first is not None:
            origin, _ = lax.optimization_barrier((me, first))
        for hop in HOPS:
            for piece in range(sub):
                distance = (hop * CLASSES + kind) * sub + piece
                target = jnp.bitwise_xor(origin, distance)
                values[distance] = lax.dynamic_slice_in_dim(features, target, 1, 0)
        if first is None:
            first = values[HOPS[0] * CLASSES * sub]
    sent = []
    results = []
    for index, kind in enumerate(ORDER):
        blocks = {}
        for order, hop in enumerate(HOPS):
            pieces = []
            for piece in range(sub):
                distance = (hop * CLASSES + kind) * sub + piece
                value = values[distance]
                if distance:
                    before = []
                    if len(sent) >= WINDOW:
                        before.append(sent[len(sent) - WINDOW])
                    if order == 0 and index >= 2:
                        before.append(results[index - 2])
                    if before:
                        value, _ = lax.optimization_barrier((value, before))
                    value = lax.ppermute(value, "space", [(i, i ^ distance) for i in range(parts)])
                    sent.append(value)
                pieces.append(value.reshape(block, channels))
            if sub == 1:
                blocks[hop] = pieces[0]
            else:
                joined = jnp.zeros((BLOCK, channels), features.dtype)
                for piece in range(sub):
                    start = jnp.bitwise_xor(me % sub, piece) * block
                    joined = lax.dynamic_update_slice(joined, pieces[piece], (start, 0))
                blocks[hop] = joined
        results.append(consume(index, [blocks[hop] for hop in range(BANDS)]))
    return results


def body(
    features,
    depth_weights,
    point_weights,
    branch_weight,
    pooling_weight,
    project_weight,
    refine_depth,
    refine_point,
):
    parts = lax.axis_size("space")
    assert features.shape[0] == parts
    block = features.shape[1]
    channels = features.shape[2]
    taps = jnp.broadcast_to(depth_weights.reshape(27, 1, channels).astype(F32), (27, 8, channels))
    refine_taps = jnp.broadcast_to(refine_depth.reshape(9, 1, HALF).astype(F32), (9, 8, HALF))
    me = lax.axis_index("space").astype(jnp.int32)
    sub = BLOCK // block
    info = jnp.stack([me // (CLASSES * sub), (me // sub) % CLASSES])
    shared = (taps, point_weights, branch_weight, project_weight)
    done = []

    def consume(index, blocks):
        if index < 3:
            done.append(class_call(info, blocks, *shared))
            return done[-1]
        return last_call(
            info, blocks, *shared, pooling_weight, [item[1] for item in done],
            [item[0] for item in done], refine_taps, refine_point
        )

    refined = exchange(features, consume)[-1]
    return lax.all_to_all(refined.reshape(parts, block, HALF), "space", 0, 0, tiled=True)


def solution(mesh):
    return jax.shard_map(
        body,
        mesh=mesh,
        in_specs=(P("dp", "space", None), P(), P(), P(), P(), P(), P(), P()),
        out_specs=P("dp", "space", None),
        check_vma=False,
    )
```

```python
import jax
import jax.numpy as jnp
from jax import lax
from jax.experimental import pallas as pl
from jax.experimental.pallas import tpu as pltpu
from jax.sharding import PartitionSpec as P

ROWS = 48
COLS = 48
RATE = 12
BANDS = ROWS // RATE
CLASSES = 4
CLASS_ROWS = RATE // CLASSES
BLOCK = CLASS_ROWS * COLS
TILE = 512
HALF = 256
LATE = 512
ORDER = (0, 1, 3, 2)
NEAR = (1, 0)
FAR = (2, 3)
F32 = jnp.float32
BF16 = jnp.bfloat16


def load_tile(info, x_refs, depth, plain, shifted, raw, taps):
    width = plain.shape[-1]
    for index in range(3):
        taps[index] = depth[index].astype(F32)

    @pl.when(pl.program_id(0) == 0)
    def _():
        shifted[:, :, 0:8, :] = jnp.zeros((BANDS, CLASS_ROWS, 8, width), F32)
        shifted[:, :, 48:56, :] = jnp.zeros((BANDS, CLASS_ROWS, 8, width), F32)

    for hop in range(BANDS):
        band = jnp.bitwise_xor(info[0], hop)
        block = x_refs[hop][...]
        raw[band] = block
        wide = block.astype(F32).reshape(CLASS_ROWS, COLS, width)
        plain[band] = wide
        shifted[band, :, 4:52, :] = wide


def spread_rows(plain, shifted, taps, spread, row, lane):
    lanes = pl.ds(lane, HALF)
    for branch in range(3):
        weights = [
            jnp.broadcast_to(taps[branch, tap:tap + 1, lanes], (8, HALF)) for tap in range(9)
        ]
        for band in range(BANDS):
            tiles = []
            for tile in range(COLS // 8):
                total = None
                for up in (-1, 0, 1):
                    source = band + up * (branch + 1)
                    if not 0 <= source < BANDS:
                        continue
                    for side in (-1, 0, 1):
                        shift = side * RATE * (branch + 1)
                        if 8 * tile + shift + 7 < 0 or 8 * tile + shift >= COLS:
                            continue
                        if shift % 8 == 0:
                            value = plain[source, row, 8 * tile + shift:8 * tile + shift + 8, lanes]
                        else:
                            start = 8 * tile + shift + 4
                            value = shifted[source, row, start:start + 8, lanes]
                        term = value * weights[3 * (up + 1) + (side + 1)]
                        total = term if total is None else total + term
                tiles.append(jnp.maximum(total, 0.0))
            sums = jnp.concatenate(tiles, axis=0).astype(BF16)
            spread[branch, band, pl.ds(pl.multiple_of(row * COLS, COLS), COLS), lanes] = sums


def pyramid_tile(info, x_refs, depth, point, branch, plain, shifted, raw, spread, taps):
    width = plain.shape[-1]
    load_tile(info, x_refs, depth, plain, shifted, raw, taps)

    def step(index, carry):
        spread_rows(plain, shifted, taps, spread, index // (width // HALF),
                    pl.multiple_of((index % (width // HALF)) * HALF, HALF))
        return carry

    lax.fori_loop(0, CLASS_ROWS * (width // HALF), step, 0)
    cells = BANDS * BLOCK
    parts = [jnp.dot(raw[...].reshape(cells, width), branch[...], preferred_element_type=F32)]
    for index in range(3):
        parts.append(
            jnp.dot(spread[index].reshape(cells, width), point[index], preferred_element_type=F32)
        )
    return parts


def accumulate(sums, parts):
    @pl.when(pl.program_id(0) == 0)
    def _():
        for index in range(4):
            sums[index] = parts[index]

    @pl.when(pl.program_id(0) > 0)
    def _():
        for index in range(4):
            sums[index] += parts[index]


def channel_sum(plain):
    width = plain.shape[-1]
    return jnp.sum(plain[...].reshape(BANDS * BLOCK // 8, 8, width), axis=0)


def pool_term(channels, pooling):
    total = channels[0]
    for item in channels[1:]:
        total = total + item
    mean = jnp.sum(total, axis=0, keepdims=True) * (1.0 / (ROWS * COLS))
    mean = jnp.broadcast_to(mean, (16, mean.shape[1])).astype(BF16)
    return jnp.dot(mean, pooling[...], preferred_element_type=F32)


def project(sums, weight):
    total = None
    for index in range(4):
        joined = jnp.maximum(sums[index], 0.0).astype(BF16)
        term = jnp.dot(
            joined, weight[HALF * index:HALF * (index + 1), :], preferred_element_type=F32
        )
        total = term if total is None else total + term
    return total


def class_kernel(info, x0, x1, x2, x3, depth, point, branch, weight, out, channel, plain, shifted,
                 raw, spread, taps, sums):
    accumulate(sums, pyramid_tile(info, (x0, x1, x2, x3), depth, point, branch, plain, shifted,
                                  raw, spread, taps))
    channel[...] = channel_sum(plain)

    @pl.when(pl.program_id(0) == pl.num_programs(0) - 1)
    def _():
        out[...] = project(sums, weight)


def early_kernel(info, x0, x1, x2, x3, depth, point, branch, pooling, channel0, channel1, channel2,
                 sums, pool, plain, shifted, raw, spread, taps):
    accumulate(sums, pyramid_tile(info, (x0, x1, x2, x3), depth, point, branch, plain, shifted,
                                  raw, spread, taps))
    term = pool_term([channel0[...], channel1[...], channel2[...], channel_sum(plain)], pooling)

    @pl.when(pl.program_id(0) == 0)
    def _():
        pool[...] = term

    @pl.when(pl.program_id(0) > 0)
    def _():
        pool[...] += term


def last_kernel(info, x0, x1, x2, x3, depth, point, branch, weight, pooling, channel0, channel1,
                channel2, sums, pool, pre0, pre1, pre2, refine_depth, refine_point, out, plain,
                shifted, raw, spread, taps, context, rows):
    parts = pyramid_tile(info, (x0, x1, x2, x3), depth, point, branch, plain, shifted, raw, spread,
                         taps)
    parts = [sums[index] + parts[index] for index in range(4)]
    term = pool_term([channel0[...], channel1[...], channel2[...], channel_sum(plain)], pooling)
    vector = jnp.maximum(pool[...] + term, 0.0).astype(BF16)
    bias = jnp.dot(vector, weight[4 * HALF:5 * HALF, :], preferred_element_type=F32)[0:1, :]
    context[0] = jnp.zeros((COLS, HALF), F32)
    context[ROWS + 1] = jnp.zeros((COLS, HALF), F32)
    pres = (pre0[...], pre1[...], pre2[...], project(parts, weight))
    for index, pre in enumerate(pres):
        first = CLASS_ROWS * jnp.bitwise_xor(info[1], ORDER[index])
        value = jnp.maximum(pre + bias, 0.0).astype(BF16).astype(F32)
        value = value.reshape(BANDS, CLASS_ROWS, COLS, HALF)
        for band in range(BANDS):
            for row in range(CLASS_ROWS):
                context[RATE * band + first + row + 1] = value[band, row]
    column = lax.broadcasted_iota(jnp.int32, (COLS, HALF), 0)
    wide = refine_depth[...].astype(F32)

    def step(row, carry):
        lines = [context[row + up] for up in range(3)]
        sides = []
        for side in range(3):
            total = None
            for up in range(3):
                term = lines[up] * wide[3 * up + side:3 * up + side + 1, :]
                total = term if total is None else total + term
            sides.append(total)
        left = jnp.where(column == 0, 0.0, pltpu.roll(sides[0], 1, 0))
        right = jnp.where(column == COLS - 1, 0.0, pltpu.roll(sides[2], COLS - 1, 0))
        total = jnp.maximum(sides[1] + left + right, 0.0).astype(BF16)
        rows[pl.ds(pl.multiple_of(row * COLS, COLS), COLS), :] = total
        return carry

    lax.fori_loop(0, ROWS, step, 0)
    product = jnp.dot(rows[...], refine_point[...], preferred_element_type=F32)
    out[...] = jnp.maximum(product, 0.0).astype(BF16)


def whole(shape):
    return pl.BlockSpec(shape, lambda i, info: (0,) * len(shape))


def pyramid_specs(blocks, start, channels):
    offset = start // TILE
    full = max(item.shape[1] for item in blocks)
    specs = []
    for item in blocks:
        first = offset if item.shape[1] == full else 0
        specs.append(pl.BlockSpec((BLOCK, TILE), lambda i, info, first=first: (0, first + i)))
    specs.append(pl.BlockSpec((3, 9, TILE), lambda i, info: (0, 0, offset + i)))
    specs.append(pl.BlockSpec((3, TILE, HALF), lambda i, info: (0, offset + i, 0)))
    specs.append(pl.BlockSpec((TILE, HALF), lambda i, info: (offset + i, 0)))
    return specs


def channel_specs(start):
    offset = start // TILE
    specs = [pl.BlockSpec((TILE, HALF), lambda i, info: (offset + i, 0))]
    return specs + [pl.BlockSpec((8, TILE), lambda i, info: (0, offset + i)) for _ in range(3)]


def pyramid_scratch():
    return [
        pltpu.VMEM((BANDS, CLASS_ROWS, COLS, TILE), F32),
        pltpu.VMEM((BANDS, CLASS_ROWS, COLS + 8, TILE), F32),
        pltpu.VMEM((BANDS, BLOCK, TILE), BF16),
        pltpu.VMEM((3, BANDS, BLOCK, TILE), BF16),
        pltpu.VMEM((3, 9, TILE), F32),
    ]


PARAMS = pltpu.CompilerParams(
    dimension_semantics=("arbitrary",), vmem_limit_bytes=52 * 1024 * 1024
)


def class_call(info, blocks, depth, point, branch, weight):
    channels = depth.shape[2]
    return pl.pallas_call(
        class_kernel,
        grid_spec=pltpu.PrefetchScalarGridSpec(
            num_scalar_prefetch=1,
            grid=(channels // TILE,),
            in_specs=pyramid_specs(blocks, 0, channels) + [whole((5 * HALF, HALF))],
            out_specs=[
                whole((BANDS * BLOCK, HALF)),
                pl.BlockSpec((8, TILE), lambda i, info: (0, i)),
            ],
            scratch_shapes=pyramid_scratch() + [pltpu.VMEM((4, BANDS * BLOCK, HALF), F32)],
        ),
        out_shape=[
            jax.ShapeDtypeStruct((BANDS * BLOCK, HALF), F32),
            jax.ShapeDtypeStruct((8, channels), F32),
        ],
        compiler_params=PARAMS,
        name="pyramid_class",
    )(info, *blocks, depth, point, branch, weight)


def early_call(info, blocks, depth, point, branch, pooling, channel):
    channels = depth.shape[2] - LATE
    return pl.pallas_call(
        early_kernel,
        grid_spec=pltpu.PrefetchScalarGridSpec(
            num_scalar_prefetch=1,
            grid=(channels // TILE,),
            in_specs=pyramid_specs(blocks, 0, channels) + channel_specs(0),
            out_specs=[whole((4, BANDS * BLOCK, HALF)), whole((16, HALF))],
            scratch_shapes=pyramid_scratch(),
        ),
        out_shape=[
            jax.ShapeDtypeStruct((4, BANDS * BLOCK, HALF), F32),
            jax.ShapeDtypeStruct((16, HALF), F32),
        ],
        compiler_params=PARAMS,
        name="pyramid_early",
    )(info, *blocks, depth, point, branch, pooling, *channel)


def last_call(info, blocks, depth, point, branch, weight, pooling, channel, sums, pool, pres,
              refine_depth, refine_point):
    start = depth.shape[2] - LATE
    specs = pyramid_specs(blocks, start, LATE) + [whole((5 * HALF, HALF))] + channel_specs(start)
    specs += [whole((4, BANDS * BLOCK, HALF)), whole((16, HALF))]
    specs += [whole((BANDS * BLOCK, HALF)) for _ in range(3)]
    specs += [whole((9, HALF)), whole((HALF, HALF))]
    return pl.pallas_call(
        last_kernel,
        grid_spec=pltpu.PrefetchScalarGridSpec(
            num_scalar_prefetch=1,
            grid=(1,),
            in_specs=specs,
            out_specs=whole((ROWS * COLS, HALF)),
            scratch_shapes=pyramid_scratch() + [
                pltpu.VMEM((ROWS + 2, COLS, HALF), F32),
                pltpu.VMEM((ROWS * COLS, HALF), BF16),
            ],
        ),
        out_shape=jax.ShapeDtypeStruct((ROWS * COLS, HALF), BF16),
        compiler_params=PARAMS,
        name="pyramid_last",
    )(info, *blocks, depth, point, branch, weight, pooling, *channel, sums, pool, *pres,
      refine_depth, refine_point)


class Sender:
    def __init__(self, features):
        self.features = features
        self.parts = lax.axis_size("space")
        self.sub = BLOCK // features.shape[1]
        self.me = lax.axis_index("space").astype(jnp.int32)
        self.values = {}
        self.far = []
        self.near = []

    def cut(self, origin, hop, kind, start, size):
        for piece in range(self.sub):
            distance = (hop * CLASSES + kind) * self.sub + piece
            target = jnp.bitwise_xor(origin, distance)
            self.values[distance, start] = lax.dynamic_slice(
                self.features, (target, 0, start), (1, self.features.shape[1], size)
            )

    def send(self, hop, kind, start, after):
        chain = self.far if hop in FAR else self.near
        got = []
        for piece in range(self.sub):
            distance = (hop * CLASSES + kind) * self.sub + piece
            value = self.values[distance, start]
            if distance:
                before = [chain[-2][piece]] if len(chain) >= 2 else []
                before += after
                if before:
                    value, _ = lax.optimization_barrier((value, before))
                value = lax.ppermute(
                    value, "space", [(i, i ^ distance) for i in range(self.parts)]
                )
            got.append(value)
        if hop or kind:
            chain.append(got)
        block, size = got[0].shape[1:]
        if self.sub == 1:
            return got[0].reshape(block, size)
        joined = jnp.zeros((BLOCK, size), value.dtype)
        for piece in range(self.sub):
            row = jnp.bitwise_xor(self.me % self.sub, piece) * block
            joined = lax.dynamic_update_slice(joined, got[piece].reshape(block, size), (row, 0))
        return joined


def body(
    features,
    depth_weights,
    point_weights,
    branch_weight,
    pooling_weight,
    project_weight,
    refine_depth,
    refine_point,
):
    parts = lax.axis_size("space")
    assert features.shape[0] == parts
    block = features.shape[1]
    channels = features.shape[2]
    send = Sender(features)
    me = send.me
    info = jnp.stack([me // (CLASSES * send.sub), (me // send.sub) % CLASSES])
    early = channels - LATE
    for hop in (2, 3, 1):
        send.cut(me, hop, ORDER[0], 0, channels)
    origin, _ = lax.optimization_barrier((me, list(send.values.values())))
    send.cut(origin, 0, ORDER[0], 0, channels)
    for kind in ORDER[1:3]:
        for hop in FAR + NEAR:
            send.cut(origin, hop, kind, 0, channels)
    for hop in FAR:
        send.cut(origin, hop, ORDER[3], 0, early)
        send.cut(origin, hop, ORDER[3], early, LATE)
    for hop in NEAR:
        send.cut(origin, hop, ORDER[3], 0, channels)
    shared = (depth_weights, point_weights, branch_weight)
    done = []
    for index in range(3):
        after = [done[index - 2]] if index >= 2 else []
        blocks = {}
        for hop in FAR + NEAR:
            blocks[hop] = send.send(hop, ORDER[index], 0, after if hop == FAR[0] else [])
        blocks = [blocks[hop] for hop in range(BANDS)]
        done.append(class_call(info, blocks, *shared, project_weight))
    pres = [item[0] for item in done]
    channel = [item[1] for item in done]
    blocks = {}
    for hop in FAR + NEAR:
        blocks[hop] = send.send(hop, ORDER[3], 0, [done[1]] if hop == FAR[0] else [])
    late = dict(blocks)
    for hop in FAR:
        late[hop] = send.send(hop, ORDER[3], early, [done[2]] if hop == FAR[0] else [])
    blocks = [blocks[hop] for hop in range(BANDS)]
    late = [late[hop] for hop in range(BANDS)]
    sums, pool = early_call(info, blocks, *shared, pooling_weight, channel)
    refined = last_call(
        info, late, *shared, project_weight, pooling_weight, channel, sums, pool, pres,
        refine_depth, refine_point
    )
    return lax.all_to_all(refined.reshape(parts, block, HALF), "space", 0, 0, tiled=True)


def solution(mesh):
    return jax.shard_map(
        body,
        mesh=mesh,
        in_specs=(P("dp", "space", None), P(), P(), P(), P(), P(), P(), P()),
        out_specs=P("dp", "space", None),
        check_vma=False,
    )
```

```python
import jax
import jax.numpy as jnp
from jax import lax
from jax.experimental import pallas as pl
from jax.experimental.pallas import tpu as pltpu
from jax.sharding import PartitionSpec as P

ROWS = 48
COLS = 48
RATE = 12
BANDS = ROWS // RATE
CLASSES = 4
CLASS_ROWS = RATE // CLASSES
BLOCK = CLASS_ROWS * COLS
TILE = 512
HALF = 256
LATE = 512
ORDER = (0, 1, 3, 2)
NEAR = (1, 0)
FAR = (2, 3)
FAR_LAG = 3
NEAR_LAG = 3
F32 = jnp.float32
BF16 = jnp.bfloat16


def load_tile(info, x_refs, depth, plain, shifted, raw, taps):
    width = plain.shape[-1]
    for index in range(3):
        taps[index] = depth[index].astype(F32)

    @pl.when(pl.program_id(0) == 0)
    def _():
        shifted[:, :, 0:8, :] = jnp.zeros((BANDS, CLASS_ROWS, 8, width), F32)
        shifted[:, :, 48:56, :] = jnp.zeros((BANDS, CLASS_ROWS, 8, width), F32)

    for hop in range(BANDS):
        band = jnp.bitwise_xor(info[0], hop)
        block = x_refs[hop][...]
        raw[band] = block
        wide = block.astype(F32).reshape(CLASS_ROWS, COLS, width)
        plain[band] = wide
        shifted[band, :, 4:52, :] = wide


def spread_branch(plain, shifted, taps, spread, branch, row, lane):
    lanes = pl.ds(lane, HALF)
    weights = [jnp.broadcast_to(taps[branch, tap:tap + 1, lanes], (8, HALF)) for tap in range(9)]
    for band in range(BANDS):
        tiles = []
        for tile in range(COLS // 8):
            total = None
            for up in (-1, 0, 1):
                source = band + up * (branch + 1)
                if not 0 <= source < BANDS:
                    continue
                for side in (-1, 0, 1):
                    shift = side * RATE * (branch + 1)
                    if 8 * tile + shift + 7 < 0 or 8 * tile + shift >= COLS:
                        continue
                    if shift % 8 == 0:
                        value = plain[source, row, 8 * tile + shift:8 * tile + shift + 8, lanes]
                    else:
                        start = 8 * tile + shift + 4
                        value = shifted[source, row, start:start + 8, lanes]
                    term = value * weights[3 * (up + 1) + (side + 1)]
                    total = term if total is None else total + term
            tiles.append(jnp.maximum(total, 0.0))
        sums = jnp.concatenate(tiles, axis=0).astype(BF16)
        spread[branch, band, row * COLS:(row + 1) * COLS, lanes] = sums


def pyramid_tile(info, x_refs, depth, point, branch, plain, shifted, raw, spread, taps):
    width = plain.shape[-1]
    load_tile(info, x_refs, depth, plain, shifted, raw, taps)
    cells = BANDS * BLOCK
    parts = [jnp.dot(raw[...].reshape(cells, width), branch[...], preferred_element_type=F32)]
    for index in range(3):
        for row in range(CLASS_ROWS):
            for lane in range(0, width, HALF):
                spread_branch(plain, shifted, taps, spread, index, row, lane)
        parts.append(
            jnp.dot(spread[index].reshape(cells, width), point[index], preferred_element_type=F32)
        )
    return parts


def accumulate(sums, parts):
    first = pl.program_id(0) == 0
    for index in range(4):
        sums[index] = jnp.where(first, 0.0, sums[index]) + parts[index]


def channel_sum(plain):
    width = plain.shape[-1]
    return jnp.sum(plain[...].reshape(BANDS * BLOCK // 8, 8, width), axis=0)


def pool_term(channels, pooling):
    total = channels[0]
    for item in channels[1:]:
        total = total + item
    mean = jnp.sum(total, axis=0, keepdims=True) * (1.0 / (ROWS * COLS))
    mean = jnp.broadcast_to(mean, (16, mean.shape[1])).astype(BF16)
    return jnp.dot(mean, pooling[...], preferred_element_type=F32)


def project(sums, weight):
    total = None
    for index in range(4):
        joined = jnp.maximum(sums[index], 0.0).astype(BF16)
        term = jnp.dot(
            joined, weight[HALF * index:HALF * (index + 1), :], preferred_element_type=F32
        )
        total = term if total is None else total + term
    return total


def class_kernel(info, x0, x1, x2, x3, depth, point, branch, weight, out, channel, plain, shifted,
                 raw, spread, taps, sums):
    accumulate(sums, pyramid_tile(info, (x0, x1, x2, x3), depth, point, branch, plain, shifted,
                                  raw, spread, taps))
    channel[...] = channel_sum(plain)

    @pl.when(pl.program_id(0) == pl.num_programs(0) - 1)
    def _():
        out[...] = project(sums, weight)


def early_kernel(info, x0, x1, x2, x3, depth, point, branch, pooling, channel0, channel1, channel2,
                 sums, pool, plain, shifted, raw, spread, taps):
    accumulate(sums, pyramid_tile(info, (x0, x1, x2, x3), depth, point, branch, plain, shifted,
                                  raw, spread, taps))
    term = pool_term([channel0[...], channel1[...], channel2[...], channel_sum(plain)], pooling)

    @pl.when(pl.program_id(0) == 0)
    def _():
        pool[...] = term

    @pl.when(pl.program_id(0) > 0)
    def _():
        pool[...] += term


def last_kernel(info, x0, x1, x2, x3, depth, point, branch, weight, pooling, channel0, channel1,
                channel2, sums, pool, pre0, pre1, pre2, refine_depth, refine_point, out, plain,
                shifted, raw, spread, taps, context, rows):
    parts = pyramid_tile(info, (x0, x1, x2, x3), depth, point, branch, plain, shifted, raw, spread,
                         taps)
    parts = [sums[index] + parts[index] for index in range(4)]
    term = pool_term([channel0[...], channel1[...], channel2[...], channel_sum(plain)], pooling)
    vector = jnp.maximum(pool[...] + term, 0.0).astype(BF16)
    bias = jnp.dot(vector, weight[4 * HALF:5 * HALF, :], preferred_element_type=F32)[0:1, :]
    context[0] = jnp.zeros((COLS, HALF), F32)
    context[ROWS + 1] = jnp.zeros((COLS, HALF), F32)
    pres = (pre0[...], pre1[...], pre2[...], project(parts, weight))
    for index, pre in enumerate(pres):
        first = CLASS_ROWS * jnp.bitwise_xor(info[1], ORDER[index])
        value = jnp.maximum(pre + bias, 0.0).astype(BF16).astype(F32)
        value = value.reshape(BANDS, CLASS_ROWS, COLS, HALF)
        for band in range(BANDS):
            for row in range(CLASS_ROWS):
                context[RATE * band + first + row + 1] = value[band, row]
    column = lax.broadcasted_iota(jnp.int32, (COLS, HALF), 0)
    wide = refine_depth[...].astype(F32)

    def step(row, carry):
        lines = [context[row + up] for up in range(3)]
        sides = []
        for side in range(3):
            total = None
            for up in range(3):
                term = lines[up] * wide[3 * up + side:3 * up + side + 1, :]
                total = term if total is None else total + term
            sides.append(total)
        left = jnp.where(column == 0, 0.0, pltpu.roll(sides[0], 1, 0))
        right = jnp.where(column == COLS - 1, 0.0, pltpu.roll(sides[2], COLS - 1, 0))
        total = jnp.maximum(sides[1] + left + right, 0.0).astype(BF16)
        rows[pl.ds(pl.multiple_of(row * COLS, COLS), COLS), :] = total
        return carry

    lax.fori_loop(0, ROWS, step, 0, unroll=4)
    product = jnp.dot(rows[...], refine_point[...], preferred_element_type=F32)
    out[...] = jnp.maximum(product, 0.0).astype(BF16)


def whole(shape):
    return pl.BlockSpec(shape, lambda i, info: (0,) * len(shape))


def pyramid_specs(blocks, start, channels):
    offset = start // TILE
    full = max(item.shape[1] for item in blocks)
    specs = []
    for item in blocks:
        first = offset if item.shape[1] == full else 0
        specs.append(pl.BlockSpec((BLOCK, TILE), lambda i, info, first=first: (0, first + i)))
    specs.append(pl.BlockSpec((3, 9, TILE), lambda i, info: (0, 0, offset + i)))
    specs.append(pl.BlockSpec((3, TILE, HALF), lambda i, info: (0, offset + i, 0)))
    specs.append(pl.BlockSpec((TILE, HALF), lambda i, info: (offset + i, 0)))
    return specs


def channel_specs(start):
    offset = start // TILE
    specs = [pl.BlockSpec((TILE, HALF), lambda i, info: (offset + i, 0))]
    return specs + [pl.BlockSpec((8, TILE), lambda i, info: (0, offset + i)) for _ in range(3)]


def pyramid_scratch():
    return [
        pltpu.VMEM((BANDS, CLASS_ROWS, COLS, TILE), F32),
        pltpu.VMEM((BANDS, CLASS_ROWS, COLS + 8, TILE), F32),
        pltpu.VMEM((BANDS, BLOCK, TILE), BF16),
        pltpu.VMEM((3, BANDS, BLOCK, TILE), BF16),
        pltpu.VMEM((3, 9, TILE), F32),
    ]


PARAMS = pltpu.CompilerParams(
    dimension_semantics=("arbitrary",), vmem_limit_bytes=52 * 1024 * 1024
)


def class_call(info, blocks, depth, point, branch, weight):
    channels = depth.shape[2]
    return pl.pallas_call(
        class_kernel,
        grid_spec=pltpu.PrefetchScalarGridSpec(
            num_scalar_prefetch=1,
            grid=(channels // TILE,),
            in_specs=pyramid_specs(blocks, 0, channels) + [whole((5 * HALF, HALF))],
            out_specs=[
                whole((BANDS * BLOCK, HALF)),
                pl.BlockSpec((8, TILE), lambda i, info: (0, i)),
            ],
            scratch_shapes=pyramid_scratch() + [pltpu.VMEM((4, BANDS * BLOCK, HALF), F32)],
        ),
        out_shape=[
            jax.ShapeDtypeStruct((BANDS * BLOCK, HALF), F32),
            jax.ShapeDtypeStruct((8, channels), F32),
        ],
        compiler_params=PARAMS,
        name="pyramid_class",
    )(info, *blocks, depth, point, branch, weight)


def early_call(info, blocks, depth, point, branch, pooling, channel):
    channels = depth.shape[2] - LATE
    return pl.pallas_call(
        early_kernel,
        grid_spec=pltpu.PrefetchScalarGridSpec(
            num_scalar_prefetch=1,
            grid=(channels // TILE,),
            in_specs=pyramid_specs(blocks, 0, channels) + channel_specs(0),
            out_specs=[whole((4, BANDS * BLOCK, HALF)), whole((16, HALF))],
            scratch_shapes=pyramid_scratch(),
        ),
        out_shape=[
            jax.ShapeDtypeStruct((4, BANDS * BLOCK, HALF), F32),
            jax.ShapeDtypeStruct((16, HALF), F32),
        ],
        compiler_params=PARAMS,
        name="pyramid_early",
    )(info, *blocks, depth, point, branch, pooling, *channel)


def last_call(info, blocks, depth, point, branch, weight, pooling, channel, sums, pool, pres,
              refine_depth, refine_point):
    start = depth.shape[2] - LATE
    specs = pyramid_specs(blocks, start, LATE) + [whole((5 * HALF, HALF))] + channel_specs(start)
    specs += [whole((4, BANDS * BLOCK, HALF)), whole((16, HALF))]
    specs += [whole((BANDS * BLOCK, HALF)) for _ in range(3)]
    specs += [whole((9, HALF)), whole((HALF, HALF))]
    return pl.pallas_call(
        last_kernel,
        grid_spec=pltpu.PrefetchScalarGridSpec(
            num_scalar_prefetch=1,
            grid=(1,),
            in_specs=specs,
            out_specs=whole((ROWS * COLS, HALF)),
            scratch_shapes=pyramid_scratch() + [
                pltpu.VMEM((ROWS + 2, COLS, HALF), F32),
                pltpu.VMEM((ROWS * COLS, HALF), BF16),
            ],
        ),
        out_shape=jax.ShapeDtypeStruct((ROWS * COLS, HALF), BF16),
        compiler_params=PARAMS,
        name="pyramid_last",
    )(info, *blocks, depth, point, branch, weight, pooling, *channel, sums, pool, *pres,
      refine_depth, refine_point)


class Sender:
    def __init__(self, features):
        self.features = features
        self.parts = lax.axis_size("space")
        self.sub = BLOCK // features.shape[1]
        self.me = lax.axis_index("space").astype(jnp.int32)
        self.values = {}
        self.far = []
        self.near = []

    def cut(self, origin, hop, kind, start, size):
        for piece in range(self.sub):
            distance = (hop * CLASSES + kind) * self.sub + piece
            target = jnp.bitwise_xor(origin, distance)
            self.values[distance, start] = lax.dynamic_slice(
                self.features, (target, 0, start), (1, self.features.shape[1], size)
            )

    def send(self, hop, kind, start, after):
        chain = self.far if hop in FAR else self.near
        got = []
        for piece in range(self.sub):
            distance = (hop * CLASSES + kind) * self.sub + piece
            value = self.values[distance, start]
            if distance:
                lag = FAR_LAG if hop in FAR else NEAR_LAG
                before = [chain[-lag][piece]] if len(chain) >= lag else []
                before += after
                if before:
                    value, _ = lax.optimization_barrier((value, before))
                value = lax.ppermute(
                    value, "space", [(i, i ^ distance) for i in range(self.parts)]
                )
            got.append(value)
        if hop or kind:
            chain.append(got)
        block, size = got[0].shape[1:]
        if self.sub == 1:
            return got[0].reshape(block, size)
        joined = jnp.zeros((BLOCK, size), value.dtype)
        for piece in range(self.sub):
            row = jnp.bitwise_xor(self.me % self.sub, piece) * block
            joined = lax.dynamic_update_slice(joined, got[piece].reshape(block, size), (row, 0))
        return joined


def body(
    features,
    depth_weights,
    point_weights,
    branch_weight,
    pooling_weight,
    project_weight,
    refine_depth,
    refine_point,
):
    parts = lax.axis_size("space")
    assert features.shape[0] == parts
    block = features.shape[1]
    channels = features.shape[2]
    send = Sender(features)
    me = send.me
    info = jnp.stack([me // (CLASSES * send.sub), (me // send.sub) % CLASSES])
    early = channels - LATE
    for hop in (2, 3, 1):
        send.cut(me, hop, ORDER[0], 0, channels)
    origin, _ = lax.optimization_barrier((me, list(send.values.values())))
    send.cut(origin, 0, ORDER[0], 0, channels)
    for kind in ORDER[1:3]:
        for hop in FAR + NEAR:
            send.cut(origin, hop, kind, 0, channels)
    for hop in FAR:
        send.cut(origin, hop, ORDER[3], 0, early)
        send.cut(origin, hop, ORDER[3], early, LATE)
    for hop in NEAR:
        send.cut(origin, hop, ORDER[3], 0, channels)
    shared = (depth_weights, point_weights, branch_weight)
    done = []
    for index in range(3):
        after = [done[index - 2]] if index >= 2 else []
        blocks = {}
        for hop in FAR + NEAR:
            blocks[hop] = send.send(hop, ORDER[index], 0, after if hop == FAR[0] else [])
        blocks = [blocks[hop] for hop in range(BANDS)]
        done.append(class_call(info, blocks, *shared, project_weight))
    pres = [item[0] for item in done]
    channel = [item[1] for item in done]
    blocks = {}
    for hop in FAR + NEAR:
        blocks[hop] = send.send(hop, ORDER[3], 0, [done[1]] if hop == FAR[0] else [])
    late = dict(blocks)
    for hop in FAR:
        late[hop] = send.send(hop, ORDER[3], early, [done[2]] if hop == FAR[1] else [])
    blocks = [blocks[hop] for hop in range(BANDS)]
    late = [late[hop] for hop in range(BANDS)]
    sums, pool = early_call(info, blocks, *shared, pooling_weight, channel)
    refined = last_call(
        info, late, *shared, project_weight, pooling_weight, channel, sums, pool, pres,
        refine_depth, refine_point
    )
    return lax.all_to_all(refined.reshape(parts, block, HALF), "space", 0, 0, tiled=True)


def solution(mesh):
    return jax.shard_map(
        body,
        mesh=mesh,
        in_specs=(P("dp", "space", None), P(), P(), P(), P(), P(), P(), P()),
        out_specs=P("dp", "space", None),
        check_vma=False,
    )
```

```python
import jax
import jax.numpy as jnp
from jax import lax
from jax.experimental import pallas as pl
from jax.experimental.pallas import tpu as pltpu
from jax.sharding import PartitionSpec as P

ROWS = 48
COLS = 48
RATE = 12
BANDS = ROWS // RATE
CLASSES = 4
CLASS_ROWS = RATE // CLASSES
BLOCK = CLASS_ROWS * COLS
TILE = 512
HALF = 256
LATE = 512
ORDER = (0, 1, 3, 2)
READY = RATE - CLASS_ROWS - 2
NEAR = (1, 0)
FAR = (2, 3)
FAR_LAG = 3
NEAR_LAG = 3
F32 = jnp.float32
BF16 = jnp.bfloat16


def load_tile(info, x_refs, depth, plain, shifted, raw, taps):
    width = plain.shape[-1]
    for index in range(3):
        taps[index] = depth[index].astype(F32)

    @pl.when(pl.program_id(0) == 0)
    def _():
        shifted[:, :, 0:8, :] = jnp.zeros((BANDS, CLASS_ROWS, 8, width), F32)
        shifted[:, :, 48:56, :] = jnp.zeros((BANDS, CLASS_ROWS, 8, width), F32)

    for hop in range(BANDS):
        band = jnp.bitwise_xor(info[0], hop)
        block = x_refs[hop][...]
        raw[band] = block
        wide = block.astype(F32).reshape(CLASS_ROWS, COLS, width)
        plain[band] = wide
        shifted[band, :, 4:52, :] = wide


def spread_branch(plain, shifted, taps, spread, branch, row, lane):
    lanes = pl.ds(lane, HALF)
    weights = [jnp.broadcast_to(taps[branch, tap:tap + 1, lanes], (8, HALF)) for tap in range(9)]
    for band in range(BANDS):
        tiles = []
        for tile in range(COLS // 8):
            total = None
            for up in (-1, 0, 1):
                source = band + up * (branch + 1)
                if not 0 <= source < BANDS:
                    continue
                for side in (-1, 0, 1):
                    shift = side * RATE * (branch + 1)
                    if 8 * tile + shift + 7 < 0 or 8 * tile + shift >= COLS:
                        continue
                    if shift % 8 == 0:
                        value = plain[source, row, 8 * tile + shift:8 * tile + shift + 8, lanes]
                    else:
                        start = 8 * tile + shift + 4
                        value = shifted[source, row, start:start + 8, lanes]
                    term = value * weights[3 * (up + 1) + (side + 1)]
                    total = term if total is None else total + term
            tiles.append(jnp.maximum(total, 0.0))
        sums = jnp.concatenate(tiles, axis=0).astype(BF16)
        spread[branch, band, row * COLS:(row + 1) * COLS, lanes] = sums


def pyramid_tile(info, x_refs, depth, point, branch, plain, shifted, raw, spread, taps):
    width = plain.shape[-1]
    load_tile(info, x_refs, depth, plain, shifted, raw, taps)
    cells = BANDS * BLOCK
    parts = [jnp.dot(raw[...].reshape(cells, width), branch[...], preferred_element_type=F32)]
    for index in range(3):
        for row in range(CLASS_ROWS):
            for lane in range(0, width, HALF):
                spread_branch(plain, shifted, taps, spread, index, row, lane)
        parts.append(
            jnp.dot(spread[index].reshape(cells, width), point[index], preferred_element_type=F32)
        )
    return parts


def accumulate(sums, parts):
    first = pl.program_id(0) == 0
    for index in range(4):
        sums[index] = jnp.where(first, 0.0, sums[index]) + parts[index]


def project(sums, weight):
    total = None
    for index in range(4):
        joined = jnp.maximum(sums[index], 0.0).astype(BF16)
        term = jnp.dot(
            joined, weight[HALF * index:HALF * (index + 1), :], preferred_element_type=F32
        )
        total = term if total is None else total + term
    return total


def context_of(sums, weight, bias):
    return jnp.maximum(project(sums, weight) + bias[...], 0.0).astype(BF16)


def place(context, info, index, value):
    first = CLASS_ROWS * jnp.bitwise_xor(info[1], ORDER[index])
    value = value.astype(F32).reshape(BANDS, CLASS_ROWS, COLS, HALF)
    for band in range(BANDS):
        for row in range(CLASS_ROWS):
            context[RATE * band + first + row + 1] = value[band, row]


def refine(info, context, rows, refine_depth, refine_point, out, first, count):
    start = CLASS_ROWS * jnp.bitwise_xor(info[1], ORDER[3]) + first + ROWS
    column = lax.broadcasted_iota(jnp.int32, (COLS, HALF), 0)
    wide = refine_depth[...].astype(F32)
    context[0] = jnp.zeros((COLS, HALF), F32)
    context[ROWS + 1] = jnp.zeros((COLS, HALF), F32)

    def place_of(index):
        return (start + RATE * (index // count) + index % count) % ROWS

    def step(index, carry):
        row = place_of(index)
        lines = [context[row + up] for up in range(3)]
        sides = []
        for side in range(3):
            total = None
            for up in range(3):
                term = lines[up] * wide[3 * up + side:3 * up + side + 1, :]
                total = term if total is None else total + term
            sides.append(total)
        left = jnp.where(column == 0, 0.0, pltpu.roll(sides[0], 1, 0))
        right = jnp.where(column == COLS - 1, 0.0, pltpu.roll(sides[2], COLS - 1, 0))
        total = jnp.maximum(sides[1] + left + right, 0.0).astype(BF16)
        rows[pl.ds(pl.multiple_of(index * COLS, COLS), COLS), :] = total
        return carry

    lax.fori_loop(0, BANDS * count, step, 0, unroll=4)
    product = jnp.dot(rows[...], refine_point[...], preferred_element_type=F32)
    product = jnp.maximum(product, 0.0).astype(BF16)
    for index in range(BANDS * count):
        place = pl.multiple_of(place_of(index) * COLS, COLS)
        out[pl.ds(place, COLS), :] = product[index * COLS:(index + 1) * COLS, :]


def class_kernel(info, x0, x1, x2, x3, depth, point, branch, weight, bias, out, plain, shifted,
                 raw, spread, taps, sums):
    accumulate(sums, pyramid_tile(info, (x0, x1, x2, x3), depth, point, branch, plain, shifted,
                                  raw, spread, taps))

    @pl.when(pl.program_id(0) == pl.num_programs(0) - 1)
    def _():
        out[...] = context_of(sums, weight, bias)


def third_kernel(info, x0, x1, x2, x3, depth, point, branch, weight, bias, context0, context1,
                 refine_depth, refine_point, out, ready, plain, shifted, raw, spread, taps, sums,
                 context, rows):
    accumulate(sums, pyramid_tile(info, (x0, x1, x2, x3), depth, point, branch, plain, shifted,
                                  raw, spread, taps))

    @pl.when(pl.program_id(0) == pl.num_programs(0) - 1)
    def _():
        value = context_of(sums, weight, bias)
        out[...] = value
        place(context, info, 0, context0[...])
        place(context, info, 1, context1[...])
        place(context, info, 2, value)
        refine(info, context, rows, refine_depth, refine_point, ready, CLASS_ROWS + 1, READY)


def early_kernel(info, x0, x1, x2, x3, depth, point, branch, sums, plain, shifted, raw, spread,
                 taps):
    accumulate(sums, pyramid_tile(info, (x0, x1, x2, x3), depth, point, branch, plain, shifted,
                                  raw, spread, taps))


def last_kernel(info, x0, x1, x2, x3, depth, point, branch, weight, bias, sums, context1, context2,
                refine_depth, refine_point, ready, out, plain, shifted, raw, spread, taps, context,
                rows):
    parts = pyramid_tile(info, (x0, x1, x2, x3), depth, point, branch, plain, shifted, raw, spread,
                         taps)
    parts = [sums[index] + parts[index] for index in range(4)]
    place(context, info, 1, context1[...])
    place(context, info, 2, context2[...])
    place(context, info, 3, context_of(parts, weight, bias))
    out[...] = ready[...]
    refine(info, context, rows, refine_depth, refine_point, out, -1, RATE - READY)


def whole(shape):
    return pl.BlockSpec(shape, lambda i, info: (0,) * len(shape))


def pyramid_specs(blocks, start, channels):
    offset = start // TILE
    full = max(item.shape[1] for item in blocks)
    specs = []
    for item in blocks:
        first = offset if item.shape[1] == full else 0
        specs.append(pl.BlockSpec((BLOCK, TILE), lambda i, info, first=first: (0, first + i)))
    specs.append(pl.BlockSpec((3, 9, TILE), lambda i, info: (0, 0, offset + i)))
    specs.append(pl.BlockSpec((3, TILE, HALF), lambda i, info: (0, offset + i, 0)))
    specs.append(pl.BlockSpec((TILE, HALF), lambda i, info: (offset + i, 0)))
    return specs


def pyramid_scratch():
    return [
        pltpu.VMEM((BANDS, CLASS_ROWS, COLS, TILE), F32),
        pltpu.VMEM((BANDS, CLASS_ROWS, COLS + 8, TILE), F32),
        pltpu.VMEM((BANDS, BLOCK, TILE), BF16),
        pltpu.VMEM((3, BANDS, BLOCK, TILE), BF16),
        pltpu.VMEM((3, 9, TILE), F32),
    ]


PARAMS = pltpu.CompilerParams(
    dimension_semantics=("arbitrary",), vmem_limit_bytes=52 * 1024 * 1024
)


SUMS = (4, BANDS * BLOCK, HALF)
CONTEXT = (BANDS * BLOCK, HALF)
IMAGE = (ROWS * COLS, HALF)


def context_scratch(count):
    return [
        pltpu.VMEM((ROWS + 2, COLS, HALF), F32),
        pltpu.VMEM((BANDS * count * COLS, HALF), BF16),
    ]


def call(kernel, name, info, blocks, weights, start, channels, extra, outs, scratch):
    specs = pyramid_specs(blocks, start, channels) + [whole(item.shape) for item in extra]
    return pl.pallas_call(
        kernel,
        grid_spec=pltpu.PrefetchScalarGridSpec(
            num_scalar_prefetch=1,
            grid=(channels // TILE,),
            in_specs=specs,
            out_specs=[whole(item.shape) for item in outs],
            scratch_shapes=pyramid_scratch() + scratch,
        ),
        out_shape=outs,
        compiler_params=PARAMS,
        name=name,
    )(info, *blocks, *weights, *extra)


class Sender:
    def __init__(self, features):
        self.features = features
        self.parts = lax.axis_size("space")
        self.sub = BLOCK // features.shape[1]
        self.me = lax.axis_index("space").astype(jnp.int32)
        self.values = {}
        self.far = []
        self.near = []

    def cut(self, origin, hop, kind, start, size):
        for piece in range(self.sub):
            distance = (hop * CLASSES + kind) * self.sub + piece
            target = jnp.bitwise_xor(origin, distance)
            self.values[distance, start] = lax.dynamic_slice(
                self.features, (target, 0, start), (1, self.features.shape[1], size)
            )

    def send(self, hop, kind, start, after):
        chain = self.far if hop in FAR else self.near
        got = []
        for piece in range(self.sub):
            distance = (hop * CLASSES + kind) * self.sub + piece
            value = self.values[distance, start]
            if distance:
                lag = FAR_LAG if hop in FAR else NEAR_LAG
                before = [chain[-lag][piece]] if len(chain) >= lag else []
                before += after
                if before:
                    value, _ = lax.optimization_barrier((value, before))
                value = lax.ppermute(
                    value, "space", [(i, i ^ distance) for i in range(self.parts)]
                )
            got.append(value)
        if hop or kind:
            chain.append(got)
        block, size = got[0].shape[1:]
        if self.sub == 1:
            return got[0].reshape(block, size)
        joined = jnp.zeros((BLOCK, size), value.dtype)
        for piece in range(self.sub):
            row = jnp.bitwise_xor(self.me % self.sub, piece) * block
            joined = lax.dynamic_update_slice(joined, got[piece].reshape(block, size), (row, 0))
        return joined


def pool_bias(features, after, pooling_weight, project_weight):
    features, _ = lax.optimization_barrier((features, after))
    cells = features.shape[1] * lax.axis_size("space")
    total = jnp.sum(features.astype(F32), axis=1)
    total = lax.psum_scatter(total, "space", scatter_dimension=0, tiled=True)
    pooled = (total / cells).astype(BF16)
    vector = jnp.dot(pooled, pooling_weight, preferred_element_type=F32)
    vector = jnp.maximum(vector, 0.0).astype(BF16)
    return jnp.dot(vector, project_weight[4 * HALF:], preferred_element_type=F32)


def body(
    features,
    depth_weights,
    point_weights,
    branch_weight,
    pooling_weight,
    project_weight,
    refine_depth,
    refine_point,
):
    parts = lax.axis_size("space")
    assert features.shape[0] == parts
    block = features.shape[1]
    channels = features.shape[2]
    send = Sender(features)
    me = send.me
    info = jnp.stack([me // (CLASSES * send.sub), (me // send.sub) % CLASSES])
    early = channels - LATE
    for hop in (2, 3, 1):
        send.cut(me, hop, ORDER[0], 0, channels)
    origin, _ = lax.optimization_barrier((me, list(send.values.values())))
    send.cut(origin, 0, ORDER[0], 0, channels)
    for kind in ORDER[1:3]:
        for hop in FAR + NEAR:
            send.cut(origin, hop, kind, 0, channels)
    for hop in FAR:
        send.cut(origin, hop, ORDER[3], 0, early)
        send.cut(origin, hop, ORDER[3], early, LATE)
    for hop in NEAR:
        send.cut(origin, hop, ORDER[3], 0, channels)
    bias = pool_bias(features, send.values[(2 * CLASSES + ORDER[1]) * send.sub, 0], pooling_weight, project_weight)
    weights = (depth_weights, point_weights, branch_weight)
    joined = project_weight[:4 * HALF]
    sums = pltpu.VMEM(SUMS, F32)
    context = jax.ShapeDtypeStruct(CONTEXT, BF16)
    image = jax.ShapeDtypeStruct(IMAGE, BF16)
    done = []
    for index in range(3):
        after = [done[index - 2]] if index >= 2 else []
        blocks = {}
        for hop in FAR + NEAR:
            blocks[hop] = send.send(hop, ORDER[index], 0, after if hop == FAR[0] else [])
        blocks = [blocks[hop] for hop in range(BANDS)]
        if index < 2:
            done += call(class_kernel, "pyramid_class", info, blocks, weights, 0, channels,
                         (joined, bias), [context], [sums])
        else:
            extra = (joined, bias, done[0], done[1], refine_depth, refine_point)
            value, ready = call(third_kernel, "pyramid_third", info, blocks, weights, 0, channels,
                                extra, [context, image], [sums] + context_scratch(READY))
            done.append(value)
    blocks = {}
    for hop in FAR + NEAR:
        blocks[hop] = send.send(hop, ORDER[3], 0, [done[1]] if hop == FAR[0] else [])
    late = dict(blocks)
    for hop in FAR:
        late[hop] = send.send(hop, ORDER[3], early, [done[2]] if hop == FAR[1] else [])
    blocks = [blocks[hop] for hop in range(BANDS)]
    late = [late[hop] for hop in range(BANDS)]
    partial, = call(early_kernel, "pyramid_early", info, blocks, weights, 0, early, (),
                    [jax.ShapeDtypeStruct(SUMS, F32)], [])
    extra = (joined, bias, partial, done[1], done[2], refine_depth, refine_point, ready)
    refined, = call(last_kernel, "pyramid_last", info, late, weights, early, LATE, extra, [image],
                    context_scratch(RATE - READY))
    return lax.all_to_all(refined.reshape(parts, block, HALF), "space", 0, 0, tiled=True)


def solution(mesh):
    return jax.shard_map(
        body,
        mesh=mesh,
        in_specs=(P("dp", "space", None), P(), P(), P(), P(), P(), P(), P()),
        out_specs=P("dp", "space", None),
        check_vma=False,
    )
```

```python
import jax
import jax.numpy as jnp
from jax import lax
from jax.experimental import pallas as pl
from jax.experimental.pallas import tpu as pltpu
from jax.sharding import PartitionSpec as P

ROWS = 48
COLS = 48
RATE = 12
BANDS = ROWS // RATE
CLASSES = 4
CLASS_ROWS = RATE // CLASSES
BLOCK = CLASS_ROWS * COLS
TILE = 512
HALF = 256
LATE = 512
ORDER = (0, 1, 3, 2)
NEAR = (1, 0)
FAR = (2, 3)
FAR_LAG = 3
NEAR_LAG = 2
F32 = jnp.float32
BF16 = jnp.bfloat16


def load_tile(info, x_refs, depth, plain, shifted, raw, taps):
    width = plain.shape[-1]
    for index in range(3):
        taps[index] = depth[index].astype(F32)

    @pl.when(pl.program_id(0) == 0)
    def _():
        shifted[:, :, 0:8, :] = jnp.zeros((BANDS, CLASS_ROWS, 8, width), F32)
        shifted[:, :, 48:56, :] = jnp.zeros((BANDS, CLASS_ROWS, 8, width), F32)

    for hop in range(BANDS):
        band = jnp.bitwise_xor(info[0], hop)
        block = x_refs[hop][...]
        raw[band] = block
        wide = block.astype(F32).reshape(CLASS_ROWS, COLS, width)
        plain[band] = wide
        shifted[band, :, 4:52, :] = wide


def spread_branch(plain, shifted, taps, spread, branch, row, lane):
    lanes = pl.ds(lane, HALF)
    weights = [jnp.broadcast_to(taps[branch, tap:tap + 1, lanes], (8, HALF)) for tap in range(9)]
    for band in range(BANDS):
        tiles = []
        for tile in range(COLS // 8):
            total = None
            for up in (-1, 0, 1):
                source = band + up * (branch + 1)
                if not 0 <= source < BANDS:
                    continue
                for side in (-1, 0, 1):
                    shift = side * RATE * (branch + 1)
                    if 8 * tile + shift + 7 < 0 or 8 * tile + shift >= COLS:
                        continue
                    if shift % 8 == 0:
                        value = plain[source, row, 8 * tile + shift:8 * tile + shift + 8, lanes]
                    else:
                        start = 8 * tile + shift + 4
                        value = shifted[source, row, start:start + 8, lanes]
                    term = value * weights[3 * (up + 1) + (side + 1)]
                    total = term if total is None else total + term
            tiles.append(jnp.maximum(total, 0.0))
        sums = jnp.concatenate(tiles, axis=0).astype(BF16)
        spread[branch, band, row * COLS:(row + 1) * COLS, lanes] = sums


def pyramid_tile(info, x_refs, depth, point, branch, plain, shifted, raw, spread, taps):
    width = plain.shape[-1]
    load_tile(info, x_refs, depth, plain, shifted, raw, taps)
    cells = BANDS * BLOCK
    parts = [jnp.dot(raw[...].reshape(cells, width), branch[...], preferred_element_type=F32)]
    for index in range(3):
        for row in range(CLASS_ROWS):
            for lane in range(0, width, HALF):
                spread_branch(plain, shifted, taps, spread, index, row, lane)
        parts.append(
            jnp.dot(spread[index].reshape(cells, width), point[index], preferred_element_type=F32)
        )
    return parts


def accumulate(sums, parts):
    first = pl.program_id(0) == 0
    for index in range(4):
        sums[index] = jnp.where(first, 0.0, sums[index]) + parts[index]


def channel_sum(plain):
    width = plain.shape[-1]
    return jnp.sum(plain[...].reshape(BANDS * BLOCK // 8, 8, width), axis=0)


def pool_term(channels, pooling):
    total = channels[0]
    for item in channels[1:]:
        total = total + item
    mean = jnp.sum(total, axis=0, keepdims=True) * (1.0 / (ROWS * COLS))
    mean = jnp.broadcast_to(mean, (16, mean.shape[1])).astype(BF16)
    return jnp.dot(mean, pooling[...], preferred_element_type=F32)


def project(sums, weight):
    total = None
    for index in range(4):
        joined = jnp.maximum(sums[index], 0.0).astype(BF16)
        term = jnp.dot(
            joined, weight[HALF * index:HALF * (index + 1), :], preferred_element_type=F32
        )
        total = term if total is None else total + term
    return total


def class_kernel(info, x0, x1, x2, x3, depth, point, branch, weight, out, channel, plain, shifted,
                 raw, spread, taps, sums):
    accumulate(sums, pyramid_tile(info, (x0, x1, x2, x3), depth, point, branch, plain, shifted,
                                  raw, spread, taps))
    channel[...] = channel_sum(plain)

    @pl.when(pl.program_id(0) == pl.num_programs(0) - 1)
    def _():
        out[...] = project(sums, weight)


def early_kernel(info, x0, x1, x2, x3, depth, point, branch, pooling, channel0, channel1, channel2,
                 sums, pool, plain, shifted, raw, spread, taps):
    accumulate(sums, pyramid_tile(info, (x0, x1, x2, x3), depth, point, branch, plain, shifted,
                                  raw, spread, taps))
    term = pool_term([channel0[...], channel1[...], channel2[...], channel_sum(plain)], pooling)

    @pl.when(pl.program_id(0) == 0)
    def _():
        pool[...] = term

    @pl.when(pl.program_id(0) > 0)
    def _():
        pool[...] += term


def last_kernel(info, x0, x1, x2, x3, depth, point, branch, weight, pooling, channel0, channel1,
                channel2, sums, pool, pre0, pre1, pre2, refine_depth, refine_point, out, plain,
                shifted, raw, spread, taps, context, rows):
    parts = pyramid_tile(info, (x0, x1, x2, x3), depth, point, branch, plain, shifted, raw, spread,
                         taps)
    parts = [sums[index] + parts[index] for index in range(4)]
    term = pool_term([channel0[...], channel1[...], channel2[...], channel_sum(plain)], pooling)
    vector = jnp.maximum(pool[...] + term, 0.0).astype(BF16)
    bias = jnp.dot(vector, weight[4 * HALF:5 * HALF, :], preferred_element_type=F32)[0:1, :]
    context[0] = jnp.zeros((COLS, HALF), F32)
    context[ROWS + 1] = jnp.zeros((COLS, HALF), F32)
    pres = (pre0[...], pre1[...], pre2[...], project(parts, weight))
    for index, pre in enumerate(pres):
        first = CLASS_ROWS * jnp.bitwise_xor(info[1], ORDER[index])
        value = jnp.maximum(pre + bias, 0.0).astype(BF16).astype(F32)
        value = value.reshape(BANDS, CLASS_ROWS, COLS, HALF)
        for band in range(BANDS):
            for row in range(CLASS_ROWS):
                context[RATE * band + first + row + 1] = value[band, row]
    column = lax.broadcasted_iota(jnp.int32, (COLS, HALF), 0)
    wide = refine_depth[...].astype(F32)

    def step(row, carry):
        lines = [context[row + up] for up in range(3)]
        sides = []
        for side in range(3):
            total = None
            for up in range(3):
                term = lines[up] * wide[3 * up + side:3 * up + side + 1, :]
                total = term if total is None else total + term
            sides.append(total)
        left = jnp.where(column == 0, 0.0, pltpu.roll(sides[0], 1, 0))
        right = jnp.where(column == COLS - 1, 0.0, pltpu.roll(sides[2], COLS - 1, 0))
        total = jnp.maximum(sides[1] + left + right, 0.0).astype(BF16)
        rows[pl.ds(pl.multiple_of(row * COLS, COLS), COLS), :] = total
        return carry

    lax.fori_loop(0, ROWS, step, 0, unroll=4)
    product = jnp.dot(rows[...], refine_point[...], preferred_element_type=F32)
    out[...] = jnp.maximum(product, 0.0).astype(BF16)


def whole(shape):
    return pl.BlockSpec(shape, lambda i, info: (0,) * len(shape))


def pyramid_specs(blocks, start, channels):
    offset = start // TILE
    full = max(item.shape[1] for item in blocks)
    specs = []
    for item in blocks:
        first = offset if item.shape[1] == full else 0
        specs.append(pl.BlockSpec((BLOCK, TILE), lambda i, info, first=first: (0, first + i)))
    specs.append(pl.BlockSpec((3, 9, TILE), lambda i, info: (0, 0, offset + i)))
    specs.append(pl.BlockSpec((3, TILE, HALF), lambda i, info: (0, offset + i, 0)))
    specs.append(pl.BlockSpec((TILE, HALF), lambda i, info: (offset + i, 0)))
    return specs


def channel_specs(start):
    offset = start // TILE
    specs = [pl.BlockSpec((TILE, HALF), lambda i, info: (offset + i, 0))]
    return specs + [pl.BlockSpec((8, TILE), lambda i, info: (0, offset + i)) for _ in range(3)]


def pyramid_scratch():
    return [
        pltpu.VMEM((BANDS, CLASS_ROWS, COLS, TILE), F32),
        pltpu.VMEM((BANDS, CLASS_ROWS, COLS + 8, TILE), F32),
        pltpu.VMEM((BANDS, BLOCK, TILE), BF16),
        pltpu.VMEM((3, BANDS, BLOCK, TILE), BF16),
        pltpu.VMEM((3, 9, TILE), F32),
    ]


PARAMS = pltpu.CompilerParams(
    dimension_semantics=("arbitrary",), vmem_limit_bytes=52 * 1024 * 1024
)


def class_call(info, blocks, depth, point, branch, weight):
    channels = depth.shape[2]
    return pl.pallas_call(
        class_kernel,
        grid_spec=pltpu.PrefetchScalarGridSpec(
            num_scalar_prefetch=1,
            grid=(channels // TILE,),
            in_specs=pyramid_specs(blocks, 0, channels) + [whole((5 * HALF, HALF))],
            out_specs=[
                whole((BANDS * BLOCK, HALF)),
                pl.BlockSpec((8, TILE), lambda i, info: (0, i)),
            ],
            scratch_shapes=pyramid_scratch() + [pltpu.VMEM((4, BANDS * BLOCK, HALF), F32)],
        ),
        out_shape=[
            jax.ShapeDtypeStruct((BANDS * BLOCK, HALF), F32),
            jax.ShapeDtypeStruct((8, channels), F32),
        ],
        compiler_params=PARAMS,
        name="pyramid_class",
    )(info, *blocks, depth, point, branch, weight)


def early_call(info, blocks, depth, point, branch, pooling, channel):
    channels = depth.shape[2] - LATE
    return pl.pallas_call(
        early_kernel,
        grid_spec=pltpu.PrefetchScalarGridSpec(
            num_scalar_prefetch=1,
            grid=(channels // TILE,),
            in_specs=pyramid_specs(blocks, 0, channels) + channel_specs(0),
            out_specs=[whole((4, BANDS * BLOCK, HALF)), whole((16, HALF))],
            scratch_shapes=pyramid_scratch(),
        ),
        out_shape=[
            jax.ShapeDtypeStruct((4, BANDS * BLOCK, HALF), F32),
            jax.ShapeDtypeStruct((16, HALF), F32),
        ],
        compiler_params=PARAMS,
        name="pyramid_early",
    )(info, *blocks, depth, point, branch, pooling, *channel)


def last_call(info, blocks, depth, point, branch, weight, pooling, channel, sums, pool, pres,
              refine_depth, refine_point):
    start = depth.shape[2] - LATE
    specs = pyramid_specs(blocks, start, LATE) + [whole((5 * HALF, HALF))] + channel_specs(start)
    specs += [whole((4, BANDS * BLOCK, HALF)), whole((16, HALF))]
    specs += [whole((BANDS * BLOCK, HALF)) for _ in range(3)]
    specs += [whole((9, HALF)), whole((HALF, HALF))]
    return pl.pallas_call(
        last_kernel,
        grid_spec=pltpu.PrefetchScalarGridSpec(
            num_scalar_prefetch=1,
            grid=(1,),
            in_specs=specs,
            out_specs=whole((ROWS * COLS, HALF)),
            scratch_shapes=pyramid_scratch() + [
                pltpu.VMEM((ROWS + 2, COLS, HALF), F32),
                pltpu.VMEM((ROWS * COLS, HALF), BF16),
            ],
        ),
        out_shape=jax.ShapeDtypeStruct((ROWS * COLS, HALF), BF16),
        compiler_params=PARAMS,
        name="pyramid_last",
    )(info, *blocks, depth, point, branch, weight, pooling, *channel, sums, pool, *pres,
      refine_depth, refine_point)


class Sender:
    def __init__(self, features):
        self.features = features
        self.parts = lax.axis_size("space")
        self.sub = BLOCK // features.shape[1]
        self.me = lax.axis_index("space").astype(jnp.int32)
        self.values = {}
        self.far = []
        self.near = []

    def cut(self, origin, hop, kind, start, size):
        for piece in range(self.sub):
            distance = (hop * CLASSES + kind) * self.sub + piece
            target = jnp.bitwise_xor(origin, distance)
            self.values[distance, start] = lax.dynamic_slice(
                self.features, (target, 0, start), (1, self.features.shape[1], size)
            )

    def send(self, hop, kind, start, after):
        chain = self.far if hop in FAR else self.near
        got = []
        for piece in range(self.sub):
            distance = (hop * CLASSES + kind) * self.sub + piece
            value = self.values[distance, start]
            if distance:
                lag = FAR_LAG if hop in FAR else NEAR_LAG
                before = [chain[-lag][piece]] if len(chain) >= lag else []
                before += after
                if before:
                    value, _ = lax.optimization_barrier((value, before))
                value = lax.ppermute(
                    value, "space", [(i, i ^ distance) for i in range(self.parts)]
                )
            got.append(value)
        if hop or kind:
            chain.append(got)
        block, size = got[0].shape[1:]
        if self.sub == 1:
            return got[0].reshape(block, size)
        joined = jnp.zeros((BLOCK, size), value.dtype)
        for piece in range(self.sub):
            row = jnp.bitwise_xor(self.me % self.sub, piece) * block
            joined = lax.dynamic_update_slice(joined, got[piece].reshape(block, size), (row, 0))
        return joined


def body(
    features,
    depth_weights,
    point_weights,
    branch_weight,
    pooling_weight,
    project_weight,
    refine_depth,
    refine_point,
):
    parts = lax.axis_size("space")
    assert features.shape[0] == parts
    block = features.shape[1]
    channels = features.shape[2]
    send = Sender(features)
    me = send.me
    info = jnp.stack([me // (CLASSES * send.sub), (me // send.sub) % CLASSES])
    early = channels - LATE
    for hop in (2, 3, 1):
        send.cut(me, hop, ORDER[0], 0, channels)
    origin, _ = lax.optimization_barrier((me, list(send.values.values())))
    send.cut(origin, 0, ORDER[0], 0, channels)
    for kind in ORDER[1:3]:
        for hop in FAR + NEAR:
            send.cut(origin, hop, kind, 0, channels)
    for hop in FAR:
        send.cut(origin, hop, ORDER[3], 0, early)
        send.cut(origin, hop, ORDER[3], early, LATE)
    for hop in NEAR:
        send.cut(origin, hop, ORDER[3], 0, channels)
    shared = (depth_weights, point_weights, branch_weight)
    done = []
    for index in range(3):
        after = [done[index - 2]] if index >= 2 else []
        blocks = {}
        for hop in FAR + NEAR:
            blocks[hop] = send.send(hop, ORDER[index], 0, after if hop == FAR[0] else [])
        blocks = [blocks[hop] for hop in range(BANDS)]
        done.append(class_call(info, blocks, *shared, project_weight))
    pres = [item[0] for item in done]
    channel = [item[1] for item in done]
    blocks = {}
    for hop in FAR + NEAR:
        blocks[hop] = send.send(hop, ORDER[3], 0, [done[1]] if hop == FAR[1] else [])
    late = dict(blocks)
    for hop in FAR:
        late[hop] = send.send(hop, ORDER[3], early, [done[2]] if hop == FAR[1] else [])
    blocks = [blocks[hop] for hop in range(BANDS)]
    late = [late[hop] for hop in range(BANDS)]
    sums, pool = early_call(info, blocks, *shared, pooling_weight, channel)
    refined = last_call(
        info, late, *shared, project_weight, pooling_weight, channel, sums, pool, pres,
        refine_depth, refine_point
    )
    return lax.all_to_all(refined.reshape(parts, block, HALF), "space", 0, 0, tiled=True)


def solution(mesh):
    return jax.shard_map(
        body,
        mesh=mesh,
        in_specs=(P("dp", "space", None), P(), P(), P(), P(), P(), P(), P()),
        out_specs=P("dp", "space", None),
        check_vma=False,
    )
```

```python
import jax
import jax.numpy as jnp
from jax import lax
from jax.experimental import pallas as pl
from jax.experimental.pallas import tpu as pltpu
from jax.sharding import PartitionSpec as P

ROWS = 48
COLS = 48
RATE = 12
BANDS = ROWS // RATE
CLASSES = 4
CLASS_ROWS = RATE // CLASSES
BLOCK = CLASS_ROWS * COLS
TILE = 512
HALF = 256
LATE = 512
ORDER = (0, 1, 3, 2)
NEAR = (1, 0)
FAR = (2, 3)
FAR_LAG = 3
NEAR_LAG = 2
F32 = jnp.float32
BF16 = jnp.bfloat16


def load_tile(info, x_refs, depth, plain, shifted, raw, taps):
    width = plain.shape[-1]
    for index in range(3):
        taps[index] = depth[index].astype(F32)

    @pl.when(pl.program_id(0) == 0)
    def _():
        shifted[:, :, 0:8, :] = jnp.zeros((BANDS, CLASS_ROWS, 8, width), F32)
        shifted[:, :, 48:56, :] = jnp.zeros((BANDS, CLASS_ROWS, 8, width), F32)

    for hop in range(BANDS):
        band = jnp.bitwise_xor(info[0], hop)
        block = x_refs[hop][...]
        raw[band] = block
        wide = block.astype(F32).reshape(CLASS_ROWS, COLS, width)
        plain[band] = wide
        shifted[band, :, 4:52, :] = wide


def spread_branch(plain, shifted, taps, spread, branch, row, lane):
    lanes = pl.ds(lane, HALF)
    weights = [jnp.broadcast_to(taps[branch, tap:tap + 1, lanes], (8, HALF)) for tap in range(9)]
    for band in range(BANDS):
        tiles = []
        for tile in range(COLS // 8):
            total = None
            for up in (-1, 0, 1):
                source = band + up * (branch + 1)
                if not 0 <= source < BANDS:
                    continue
                for side in (-1, 0, 1):
                    shift = side * RATE * (branch + 1)
                    if 8 * tile + shift + 7 < 0 or 8 * tile + shift >= COLS:
                        continue
                    if shift % 8 == 0:
                        value = plain[source, row, 8 * tile + shift:8 * tile + shift + 8, lanes]
                    else:
                        start = 8 * tile + shift + 4
                        value = shifted[source, row, start:start + 8, lanes]
                    term = value * weights[3 * (up + 1) + (side + 1)]
                    total = term if total is None else total + term
            tiles.append(jnp.maximum(total, 0.0))
        sums = jnp.concatenate(tiles, axis=0).astype(BF16)
        spread[branch, band, row * COLS:(row + 1) * COLS, lanes] = sums


def pyramid_tile(info, x_refs, depth, point, branch, plain, shifted, raw, spread, taps):
    width = plain.shape[-1]
    load_tile(info, x_refs, depth, plain, shifted, raw, taps)
    cells = BANDS * BLOCK
    parts = [jnp.dot(raw[...].reshape(cells, width), branch[...], preferred_element_type=F32)]
    for index in range(3):
        for row in range(CLASS_ROWS):
            for lane in range(0, width, HALF):
                spread_branch(plain, shifted, taps, spread, index, row, lane)
        parts.append(
            jnp.dot(spread[index].reshape(cells, width), point[index], preferred_element_type=F32)
        )
    return parts


def accumulate(sums, parts):
    first = pl.program_id(0) == 0
    for index in range(4):
        sums[index] = jnp.where(first, 0.0, sums[index]) + parts[index]


def channel_sum(plain):
    width = plain.shape[-1]
    return jnp.sum(plain[...].reshape(BANDS * BLOCK // 8, 8, width), axis=0)


def pool_term(channels, pooling):
    total = channels[0]
    for item in channels[1:]:
        total = total + item
    mean = jnp.sum(total, axis=0, keepdims=True) * (1.0 / (ROWS * COLS))
    mean = jnp.broadcast_to(mean, (16, mean.shape[1])).astype(BF16)
    return jnp.dot(mean, pooling[...], preferred_element_type=F32)


def project(sums, weight):
    total = None
    for index in range(4):
        joined = jnp.maximum(sums[index], 0.0).astype(BF16)
        term = jnp.dot(
            joined, weight[HALF * index:HALF * (index + 1), :], preferred_element_type=F32
        )
        total = term if total is None else total + term
    return total


def class_kernel(info, x0, x1, x2, x3, depth, point, branch, weight, out, channel, plain, shifted,
                 raw, spread, taps, sums):
    accumulate(sums, pyramid_tile(info, (x0, x1, x2, x3), depth, point, branch, plain, shifted,
                                  raw, spread, taps))
    channel[...] = channel_sum(plain)

    @pl.when(pl.program_id(0) == pl.num_programs(0) - 1)
    def _():
        out[...] = project(sums, weight)


def early_kernel(info, x0, x1, x2, x3, depth, point, branch, pooling, channel0, channel1, channel2,
                 sums, pool, plain, shifted, raw, spread, taps):
    accumulate(sums, pyramid_tile(info, (x0, x1, x2, x3), depth, point, branch, plain, shifted,
                                  raw, spread, taps))
    term = pool_term([channel0[...], channel1[...], channel2[...], channel_sum(plain)], pooling)

    @pl.when(pl.program_id(0) == 0)
    def _():
        pool[...] = term

    @pl.when(pl.program_id(0) > 0)
    def _():
        pool[...] += term


def last_kernel(info, x0, x1, x2, x3, depth, point, branch, weight, pooling, channel0, channel1,
                channel2, sums_in, pool, pre0, pre1, pre2, refine_depth, refine_point, out, plain,
                shifted, raw, spread, taps, context, rows, sums, pres, arrived):
    copies = [pltpu.make_async_copy(sums_in, sums, arrived.at[3])]
    for index, item in enumerate((pre0, pre1, pre2)):
        copies.append(pltpu.make_async_copy(item, pres.at[index], arrived.at[index]))
    for item in copies:
        item.start()
    parts = pyramid_tile(info, (x0, x1, x2, x3), depth, point, branch, plain, shifted, raw, spread,
                         taps)
    term = pool_term([channel0[...], channel1[...], channel2[...], channel_sum(plain)], pooling)
    vector = jnp.maximum(pool[...] + term, 0.0).astype(BF16)
    bias = jnp.dot(vector, weight[4 * HALF:5 * HALF, :], preferred_element_type=F32)[0:1, :]
    context[0] = jnp.zeros((COLS, HALF), F32)
    context[ROWS + 1] = jnp.zeros((COLS, HALF), F32)
    for item in copies:
        item.wait()
    last = project([sums[index] + parts[index] for index in range(4)], weight)
    for index in range(4):
        first = CLASS_ROWS * jnp.bitwise_xor(info[1], ORDER[index])
        for band in range(BANDS):
            for row in range(CLASS_ROWS):
                start = COLS * (CLASS_ROWS * band + row)
                value = pres[index, start:start + COLS, :] if index < 3 else last[start:start + COLS, :]
                value = jnp.maximum(value + bias, 0.0).astype(BF16).astype(F32)
                context[RATE * band + first + row + 1] = value
    column = lax.broadcasted_iota(jnp.int32, (COLS, HALF), 0)
    wide = refine_depth[...].astype(F32)

    def step(row, carry):
        lines = [context[row + up] for up in range(3)]
        sides = []
        for side in range(3):
            total = None
            for up in range(3):
                term = lines[up] * wide[3 * up + side:3 * up + side + 1, :]
                total = term if total is None else total + term
            sides.append(total)
        left = jnp.where(column == 0, 0.0, pltpu.roll(sides[0], 1, 0))
        right = jnp.where(column == COLS - 1, 0.0, pltpu.roll(sides[2], COLS - 1, 0))
        total = jnp.maximum(sides[1] + left + right, 0.0).astype(BF16)
        rows[pl.ds(pl.multiple_of(row * COLS, COLS), COLS), :] = total
        return carry

    lax.fori_loop(0, ROWS, step, 0, unroll=4)
    product = jnp.dot(rows[...], refine_point[...], preferred_element_type=F32)
    out[...] = jnp.maximum(product, 0.0).astype(BF16)


def whole(shape):
    return pl.BlockSpec(shape, lambda i, info: (0,) * len(shape))


def pyramid_specs(blocks, start, channels):
    offset = start // TILE
    full = max(item.shape[1] for item in blocks)
    specs = []
    for item in blocks:
        first = offset if item.shape[1] == full else 0
        specs.append(pl.BlockSpec((BLOCK, TILE), lambda i, info, first=first: (0, first + i)))
    specs.append(pl.BlockSpec((3, 9, TILE), lambda i, info: (0, 0, offset + i)))
    specs.append(pl.BlockSpec((3, TILE, HALF), lambda i, info: (0, offset + i, 0)))
    specs.append(pl.BlockSpec((TILE, HALF), lambda i, info: (offset + i, 0)))
    return specs


def channel_specs(start):
    offset = start // TILE
    specs = [pl.BlockSpec((TILE, HALF), lambda i, info: (offset + i, 0))]
    return specs + [pl.BlockSpec((8, TILE), lambda i, info: (0, offset + i)) for _ in range(3)]


def pyramid_scratch():
    return [
        pltpu.VMEM((BANDS, CLASS_ROWS, COLS, TILE), F32),
        pltpu.VMEM((BANDS, CLASS_ROWS, COLS + 8, TILE), F32),
        pltpu.VMEM((BANDS, BLOCK, TILE), BF16),
        pltpu.VMEM((3, BANDS, BLOCK, TILE), BF16),
        pltpu.VMEM((3, 9, TILE), F32),
    ]


PARAMS = pltpu.CompilerParams(
    dimension_semantics=("arbitrary",), vmem_limit_bytes=32 * 1024 * 1024
)


def class_call(info, blocks, depth, point, branch, weight):
    channels = depth.shape[2]
    return pl.pallas_call(
        class_kernel,
        grid_spec=pltpu.PrefetchScalarGridSpec(
            num_scalar_prefetch=1,
            grid=(channels // TILE,),
            in_specs=pyramid_specs(blocks, 0, channels) + [whole((5 * HALF, HALF))],
            out_specs=[
                whole((BANDS * BLOCK, HALF)),
                pl.BlockSpec((8, TILE), lambda i, info: (0, i)),
            ],
            scratch_shapes=pyramid_scratch() + [pltpu.VMEM((4, BANDS * BLOCK, HALF), F32)],
        ),
        out_shape=[
            jax.ShapeDtypeStruct((BANDS * BLOCK, HALF), F32),
            jax.ShapeDtypeStruct((8, channels), F32),
        ],
        compiler_params=PARAMS,
        name="pyramid_class",
    )(info, *blocks, depth, point, branch, weight)


def early_call(info, blocks, depth, point, branch, pooling, channel):
    channels = depth.shape[2] - LATE
    return pl.pallas_call(
        early_kernel,
        grid_spec=pltpu.PrefetchScalarGridSpec(
            num_scalar_prefetch=1,
            grid=(channels // TILE,),
            in_specs=pyramid_specs(blocks, 0, channels) + channel_specs(0),
            out_specs=[whole((4, BANDS * BLOCK, HALF)), whole((16, HALF))],
            scratch_shapes=pyramid_scratch(),
        ),
        out_shape=[
            jax.ShapeDtypeStruct((4, BANDS * BLOCK, HALF), F32),
            jax.ShapeDtypeStruct((16, HALF), F32),
        ],
        compiler_params=PARAMS,
        name="pyramid_early",
    )(info, *blocks, depth, point, branch, pooling, *channel)


def last_call(info, blocks, depth, point, branch, weight, pooling, channel, sums, pool, pres,
              refine_depth, refine_point):
    start = depth.shape[2] - LATE
    specs = pyramid_specs(blocks, start, LATE) + [whole((5 * HALF, HALF))] + channel_specs(start)
    specs += [pl.BlockSpec(memory_space=pl.ANY), whole((16, HALF))]
    specs += [pl.BlockSpec(memory_space=pl.ANY) for _ in range(3)]
    specs += [whole((9, HALF)), whole((HALF, HALF))]
    return pl.pallas_call(
        last_kernel,
        grid_spec=pltpu.PrefetchScalarGridSpec(
            num_scalar_prefetch=1,
            grid=(1,),
            in_specs=specs,
            out_specs=whole((ROWS * COLS, HALF)),
            scratch_shapes=pyramid_scratch() + [
                pltpu.VMEM((ROWS + 2, COLS, HALF), F32),
                pltpu.VMEM((ROWS * COLS, HALF), BF16),
                pltpu.VMEM((4, BANDS * BLOCK, HALF), F32),
                pltpu.VMEM((3, BANDS * BLOCK, HALF), F32),
                pltpu.SemaphoreType.DMA((4,)),
            ],
        ),
        out_shape=jax.ShapeDtypeStruct((ROWS * COLS, HALF), BF16),
        compiler_params=PARAMS,
        name="pyramid_last",
    )(info, *blocks, depth, point, branch, weight, pooling, *channel, sums, pool, *pres,
      refine_depth, refine_point)


class Sender:
    def __init__(self, features):
        self.features = features
        self.parts = lax.axis_size("space")
        self.sub = BLOCK // features.shape[1]
        self.me = lax.axis_index("space").astype(jnp.int32)
        self.values = {}
        self.far = []
        self.near = []

    def cut(self, origin, hop, kind, start, size):
        for piece in range(self.sub):
            distance = (hop * CLASSES + kind) * self.sub + piece
            target = jnp.bitwise_xor(origin, distance)
            self.values[distance, start] = lax.dynamic_slice(
                self.features, (target, 0, start), (1, self.features.shape[1], size)
            )

    def send(self, hop, kind, start, after):
        chain = self.far if hop in FAR else self.near
        got = []
        for piece in range(self.sub):
            distance = (hop * CLASSES + kind) * self.sub + piece
            value = self.values[distance, start]
            if distance:
                lag = FAR_LAG if hop in FAR else NEAR_LAG
                before = [chain[-lag][piece]] if len(chain) >= lag else []
                before += after
                if before:
                    value, _ = lax.optimization_barrier((value, before))
                value = lax.ppermute(
                    value, "space", [(i, i ^ distance) for i in range(self.parts)]
                )
            got.append(value)
        if hop or kind:
            chain.append(got)
        block, size = got[0].shape[1:]
        if self.sub == 1:
            return got[0].reshape(block, size)
        joined = jnp.zeros((BLOCK, size), value.dtype)
        for piece in range(self.sub):
            row = jnp.bitwise_xor(self.me % self.sub, piece) * block
            joined = lax.dynamic_update_slice(joined, got[piece].reshape(block, size), (row, 0))
        return joined


def body(
    features,
    depth_weights,
    point_weights,
    branch_weight,
    pooling_weight,
    project_weight,
    refine_depth,
    refine_point,
):
    parts = lax.axis_size("space")
    assert features.shape[0] == parts
    block = features.shape[1]
    channels = features.shape[2]
    send = Sender(features)
    me = send.me
    info = jnp.stack([me // (CLASSES * send.sub), (me // send.sub) % CLASSES])
    early = channels - LATE
    for hop in (2, 3, 1):
        send.cut(me, hop, ORDER[0], 0, channels)
    origin, _ = lax.optimization_barrier((me, list(send.values.values())))
    send.cut(origin, 0, ORDER[0], 0, channels)
    for kind in ORDER[1:3]:
        for hop in FAR + NEAR:
            send.cut(origin, hop, kind, 0, channels)
    for hop in FAR:
        send.cut(origin, hop, ORDER[3], 0, early)
        send.cut(origin, hop, ORDER[3], early, LATE)
    for hop in NEAR:
        send.cut(origin, hop, ORDER[3], 0, channels)
    shared = (depth_weights, point_weights, branch_weight)
    done = []
    for index in range(3):
        after = [done[index - 2]] if index >= 2 else []
        blocks = {}
        for hop in FAR + NEAR:
            blocks[hop] = send.send(hop, ORDER[index], 0, after if hop == FAR[0] else [])
        blocks = [blocks[hop] for hop in range(BANDS)]
        done.append(class_call(info, blocks, *shared, project_weight))
    pres = [item[0] for item in done]
    channel = [item[1] for item in done]
    blocks = {}
    for hop in FAR + NEAR:
        blocks[hop] = send.send(hop, ORDER[3], 0, [done[1]] if hop == FAR[1] else [])
    late = dict(blocks)
    for hop in FAR:
        late[hop] = send.send(hop, ORDER[3], early, [done[2]] if hop == FAR[1] else [])
    blocks = [blocks[hop] for hop in range(BANDS)]
    late = [late[hop] for hop in range(BANDS)]
    sums, pool = early_call(info, blocks, *shared, pooling_weight, channel)
    refined = last_call(
        info, late, *shared, project_weight, pooling_weight, channel, sums, pool, pres,
        refine_depth, refine_point
    )
    return lax.all_to_all(refined.reshape(parts, block, HALF), "space", 0, 0, tiled=True)


def solution(mesh):
    return jax.shard_map(
        body,
        mesh=mesh,
        in_specs=(P("dp", "space", None), P(), P(), P(), P(), P(), P(), P()),
        out_specs=P("dp", "space", None),
        check_vma=False,
    )
```
